32 devices in a mesh: cls: 4 (over x, core), lvl: 8 (over z, y).
Axes of the slice: x: 2, y: 2, z: 4, core: 2. Of those that a mesh axis runs over, the one named last changes fastest.
Arguments:
- occupancy: float32 [8, 256, 256, 256], P('lvl', 'cls'), may hold values from 0.1 to 10
- rates: float32 [3, 256, 256], replicated, may hold values from 0.01 to 1
- increments: int32 [3, 256], replicated, may hold values from 0 to 1
- draw: int32 [256], replicated, may hold values from 1 to 2
- crusher_rate: float32 [256], replicated, may hold values from 2 to 60
- bounds: int32 [2], replicated, may hold values from -2 to 8, as said below
Outputs:
- new_occupancy: float32 [8, 256, 256, 256], P('lvl', 'cls')
The draws below stay inside these ranges and needn't reach their ends.
Inputs may be any that keep to these rules, and one draw needn't show every extreme that they name: bounds[0] is at most 0 and bounds[1] is at least 7.
All inputs are finite; a program needn't handle non-finite values.
Results may differ from the reference program's by a relative error of at most 0.0003.
Values sent between devices are 32-bit elements; how exact they have to be, the bound alone decides.
No kernel may reach another device: no remote copies, remote signals or barrier semaphores. Data moves between devices by JAX's collectives and lax.ppermute only.
A program may use at most 320 MiB of HBM per device.

```python
import math
import jax
import jax.numpy as jnp
from jax import lax

P_SIZE = 256
STEPS = 1
NL = 8


def draw_bounds(key, part):
    first = jax.random.fold_in(key, 11)
    second = jax.random.fold_in(key, 23)
    lowest = jax.random.randint(first, (1,), -2, 1)
    highest = NL - 1 + jax.random.randint(second, (1,), 0, 2)
    return jnp.concatenate([lowest, highest]).astype(jnp.int32)


def set_ends(result, own_key, low, top_value):
    spot = [jax.random.randint(jax.random.fold_in(own_key, axis), (), 0, length) for axis, length in enumerate(result.shape)]
    longest = result.shape.index(max(result.shape))
    neighbour = spot[:longest] + [(spot[longest] + 1) % result.shape[longest]] + spot[longest + 1:]
    return result.at[tuple(spot)].set(low).at[tuple(neighbour)].set(top_value)


def shard_levels(own_key, shape, shards, low, high):
    factor_of, own = 1.0, jax.random.fold_in(own_key, 6)
    for axis_at, blocks in shards:
        draws = jnp.exp(jax.random.uniform(jax.random.fold_in(own, axis_at), (blocks,), jnp.float32, low / len(shards), high / len(shards)))
        factor_of = factor_of * jnp.repeat(draws, shape[axis_at] // blocks).reshape([-1 if axis == axis_at else 1 for axis in range(len(shape))])
    return factor_of


def setup_inputs(seed: int = 0) -> dict:
    seeds = jax.random.split(jax.random.key(seed), 7)
    return {
        "occupancy": jnp.clip(jnp.exp(math.log(10.0) - 4.6051702 * jax.random.uniform(seeds[0], (NL, P_SIZE, P_SIZE, P_SIZE), jnp.float32) ** shard_levels(seeds[0], (NL, P_SIZE, P_SIZE, P_SIZE), ((0, 8), (1, 4)), -0.2, 0.2)), 0.1, 10.0),
        "rates": jnp.clip(jnp.exp(jax.random.uniform(seeds[1], (3, P_SIZE, P_SIZE), jnp.float32, math.log(0.01), math.log(1.0))), 0.01, 1.0),
        "increments": set_ends(jax.random.randint(seeds[2], (3, P_SIZE), 0, 2), jax.random.fold_in(seeds[2], 1), 0, 1).astype(jnp.int32),
        "draw": set_ends(jax.random.randint(seeds[3], (P_SIZE,), 1, 3), jax.random.fold_in(seeds[3], 1), 1, 2).astype(jnp.int32),
        "crusher_rate": jnp.clip(jnp.exp(jax.random.uniform(seeds[4], (P_SIZE,), jnp.float32, math.log(2.0), math.log(60.0))), 2.0, 60.0),
        "bounds": draw_bounds(jax.random.fold_in(seeds[6], 71), 0),
    }


def paired(rates_k, inc_k):
    stay_rows = rates_k * jnp.where(inc_k == 0, 1.0, 0.0).astype(rates_k.dtype)[:, None]
    rise_rows = rates_k * jnp.where(inc_k == 1, 1.0, 0.0).astype(rates_k.dtype)[:, None]
    return jnp.concatenate([stay_rows, rise_rows], axis=1)


def reference(occupancy, rates, increments, draw, crusher_rate, bounds):
    bottom = bounds[0]
    top = bounds[1]
    row_total = jnp.sum(rates, axis=2)
    uniform_rate = jnp.sum(jnp.max(row_total, axis=1)) + jnp.max(crusher_rate)
    cat_a = paired(rates[0], increments[0])
    cat_b = paired(rates[1], increments[1])
    cat_c = paired(rates[2], increments[2])
    highest = lax.Precision.HIGHEST
    ftype = occupancy.dtype

    def flag(cond):
        return jnp.where(cond, 1.0, 0.0).astype(ftype)

    def fall_from(state, source, depth):
        safe = jnp.minimum(source, NL - 1).astype(jnp.int32)
        piece = lax.dynamic_index_in_dim(state, safe, 0, keepdims=False)
        factor = crusher_rate * flag(draw == depth) * flag(source - draw >= bottom) * flag(source < NL)
        return piece * factor[None, None, :]

    def one_step(state):
        def level_fn(carry, level):
            here = lax.dynamic_index_in_dim(state, level, 0, keepdims=False)
            both_a = jnp.einsum('abc,ax->xbc', here, cat_a, precision=highest)
            both_b = jnp.einsum('abc,bx->axc', here, cat_b, precision=highest)
            both_c = jnp.einsum('abc,cx->abx', here, cat_c, precision=highest)
            stay = both_a[:P_SIZE] + both_b[:, :P_SIZE] + both_c[:, :, :P_SIZE]
            rise = (both_a[P_SIZE:] + both_b[:, P_SIZE:] + both_c[:, :, P_SIZE:]) * flag(level + 1 <= top)
            opened = flag((increments == 0) | (level + increments <= top))
            out_rows = row_total * opened
            drop_ok = flag(level - draw >= bottom)
            outflow = out_rows[0][:, None, None] + out_rows[1][None, :, None] + (out_rows[2] + crusher_rate * drop_ok)[None, None, :]
            fall = fall_from(state, level + 1, 1) + fall_from(state, level + 2, 2)
            fresh = here + (stay + carry + fall - outflow * here) / uniform_rate
            return rise, fresh

        init = jnp.zeros((P_SIZE, P_SIZE, P_SIZE), jnp.float32)
        _, levels = lax.scan(level_fn, init, jnp.arange(NL, dtype=jnp.int32))
        return levels

    state = occupancy
    for step in range(STEPS):
        state = one_step(state)
    return state
```

```python
import functools

import jax
import jax.numpy as jnp
from jax import lax
from jax.experimental import pallas as pl
from jax.experimental.pallas import tpu as pltpu
from jax.sharding import PartitionSpec as P

F32 = jnp.float32
BF16 = jnp.bfloat16
VMEM_LIMIT = 56 * 2**20


def flag(cond):
    return jnp.where(cond, 1.0, 0.0).astype(F32)


def halves(x):
    high = x.astype(BF16)
    low = (x - high.astype(F32)).astype(BF16)
    return high, low


def halves_outside(x):
    high = lax.reduce_precision(x, 8, 7)
    return high.astype(BF16), (x - high).astype(BF16)


def dot(a, b):
    return jnp.dot(a, b, preferred_element_type=F32)


def chunk_bounds(length):
    unit = length // 32
    sizes = [1, 2, 3, 4, 4, 4, 4, 4, 3, 2, 1]
    starts, at = [], 0
    for size in sizes:
        starts.append((at * unit, size * unit))
        at += size
    assert at == 32
    return starts


def local_kernel(own_rows, occ, c_hi, c_lo, b_hi, b_lo, row_b, row_c, base, rise):
    block, phases = occ.shape[0], occ.shape[2]
    first = pl.program_id(0) * block
    for i in range(block):
        x = occ[i]
        x_hi, x_lo = halves(x)
        by_c = dot(x_hi, c_hi[...]) + dot(x_lo, c_hi[...]) + dot(x_hi, c_lo[...])
        by_b = dot(b_hi[...], x_hi) + dot(b_hi[...], x_lo) + dot(b_lo[...], x_hi)
        left = row_c[...] - own_rows[first + i] - row_b[...]
        base[i] = by_c[:, :phases] + by_b[: x.shape[0]] + x * left
        rise[i] = by_c[:, phases:] + by_b[x.shape[0] :]


def local_terms(occ, own_rows, cat_c, cat_b_t, row_b, row_c):
    rows, mid, phases = occ.shape
    block = 4
    c_hi, c_lo = halves_outside(cat_c)
    b_hi, b_lo = halves_outside(cat_b_t)
    whole = pl.BlockSpec(memory_space=pltpu.VMEM)
    slab = pl.BlockSpec((block, mid, phases), lambda i: (i, 0, 0))
    return pl.pallas_call(
        local_kernel,
        grid=(rows // block,),
        in_specs=[pl.BlockSpec(memory_space=pltpu.SMEM), slab] + [whole] * 6,
        out_specs=[slab, slab],
        out_shape=[jax.ShapeDtypeStruct(occ.shape, F32)] * 2,
        compiler_params=pltpu.CompilerParams(vmem_limit_bytes=VMEM_LIMIT),
        cost_estimate=pl.CostEstimate(
            flops=rows * mid * phases * phases * 24, transcendentals=0, bytes_accessed=occ.size * 12
        ),
        name="local_terms",
    )(own_rows, occ, c_hi, c_lo, b_hi, b_lo, row_b, row_c)


def first_kernel(n_slabs, *refs):
    w_both, w_hi = refs[0], refs[1]
    slabs = refs[2 : 2 + n_slabs]
    base, rise_in, stay_out, rise_out = refs[2 + n_slabs :]
    rows, span, lanes = base.shape
    flat = [ref.reshape(rows * span, lanes) for ref in slabs]
    stay_flat = stay_out.reshape(rows * span, lanes)
    rise_flat = rise_out.reshape(rows * span, lanes)
    for b in range(0, span, 2):
        ats = [pl.ds(b, rows, stride=span), pl.ds(b + 1, rows, stride=span)]
        parts = [halves(jnp.concatenate([ref[at, :] for at in ats], axis=1)) for ref in flat]
        g_hi = jnp.concatenate([p[0] for p in parts], axis=0)
        g_lo = jnp.concatenate([p[1] for p in parts], axis=0)
        both = dot(w_both[...], g_hi)
        out = both[: 2 * rows] + both[2 * rows :] + dot(w_hi[...], g_lo)
        for n, at in enumerate(ats):
            stay_flat[at, :] = out[:rows, n * lanes : (n + 1) * lanes]
            rise_flat[at, :] = out[rows:, n * lanes : (n + 1) * lanes]
    stay_out[...] += base[...]
    rise_out[...] += rise_in[...]


def first_terms(w_both, w_hi, slabs, base, rise, start, size):
    rows, _, phases = base.shape
    span, lanes = 8, 128

    def at(offset):
        return pl.BlockSpec((rows, span, lanes), lambda j, h: (0, offset // span + j, h))

    whole = pl.BlockSpec(memory_space=pltpu.VMEM)
    n = len(slabs)
    return pl.pallas_call(
        functools.partial(first_kernel, n),
        grid=(size // span, phases // lanes),
        in_specs=[whole, whole] + [at(off) for _, off in slabs] + [at(start), at(start)],
        out_specs=[at(0), at(0)],
        out_shape=[jax.ShapeDtypeStruct((rows, size, phases), F32)] * 2,
        compiler_params=pltpu.CompilerParams(vmem_limit_bytes=VMEM_LIMIT),
        cost_estimate=pl.CostEstimate(
            flops=6 * 2 * rows * rows * n * size * phases,
            transcendentals=0,
            bytes_accessed=rows * size * phases * 4 * (n + 4),
        ),
        name="first_terms",
    )(w_both, w_hi, *[a for a, _ in slabs], base, rise)


def finish_kernel(scale, stay, fall, risen, deep, *refs):
    out = refs[-1]
    out[...] = (stay[...] + risen[...] + fall[...] * deep[...]) * scale[0]


def finish(out, shape, scale, stay, fall, risen, deep, start, size):
    rows, _, phases = shape
    span = 8
    chunk = pl.BlockSpec((rows, span, phases), lambda j: (0, j, 0))
    args = [scale, stay, fall, risen, deep]
    specs = [pl.BlockSpec(memory_space=pltpu.SMEM), chunk, pl.BlockSpec(memory_space=pltpu.VMEM), chunk, chunk]
    alias = {}
    if out is not None:
        args.append(out)
        specs.append(pl.BlockSpec(memory_space=pl.ANY))
        alias = {5: 0}
    return pl.pallas_call(
        finish_kernel,
        grid=(size // span,),
        in_specs=specs,
        out_specs=pl.BlockSpec((rows, span, phases), lambda j: (0, start // span + j, 0)),
        out_shape=jax.ShapeDtypeStruct(shape, F32),
        input_output_aliases=alias,
        compiler_params=pltpu.CompilerParams(vmem_limit_bytes=VMEM_LIMIT),
        cost_estimate=pl.CostEstimate(
            flops=3 * rows * size * phases, transcendentals=0, bytes_accessed=rows * size * phases * 16
        ),
        name="finish",
    )(*args)


def local(occupancy, rates, increments, draw, crusher_rate, bounds):
    n_cls, n_lvl = lax.axis_size("cls"), lax.axis_size("lvl")
    occ = occupancy[0]
    rows, mid, phases = occ.shape
    level = lax.axis_index("lvl")
    place = lax.axis_index("cls")
    even = level % 2 == 0
    bottom, top = bounds[0], bounds[1]

    row_total = jnp.sum(rates, axis=2)
    uniform_rate = jnp.sum(jnp.max(row_total, axis=1)) + jnp.max(crusher_rate)
    out_rows = row_total * flag((increments == 0) | (level + increments <= top))
    rise_ok = flag(level + 1 <= top)
    drop_here = crusher_rate * flag(level - draw >= bottom)
    drop_deep = crusher_rate * flag(level + 2 - draw >= bottom)
    once_here = (drop_here * flag(draw == 1) * flag(~even))[None, None, :]
    once_deep = (drop_deep * flag(draw == 1) * flag(even))[None, None, :]
    twice_deep = (drop_deep * flag(draw == 2))[None, :]

    stay_rows = rates * flag(increments == 0)[:, :, None]
    rise_rows = rates * (flag(increments == 1) * rise_ok)[:, :, None]

    def along_cls(v, by):
        return lax.ppermute(v, "cls", [(i, (i + by) % n_cls) for i in range(n_cls)])

    def other_core(v):
        return lax.ppermute(v, "cls", [(i, i ^ 1) for i in range(n_cls)])

    def two_down(v):
        return lax.ppermute(v, "lvl", [(i, i - 2) for i in range(2, n_lvl)])

    def two_up(v):
        return lax.ppermute(v, "lvl", [(i, i + 2) for i in range(1, n_lvl - 2, 2)])

    def pair_swap(v):
        return lax.ppermute(v, "lvl", [(i, i ^ 1) for i in range(n_lvl)])

    chunks = chunk_bounds(mid)
    shifts = [2 * s for s in range(1, n_cls // 2)]
    sent = [lax.slice_in_dim(occ, at, at + size, axis=1) for at, size in chunks]
    far = [[along_cls(v, by) for by in shifts] for v in sent]
    deep = [two_down(v) for v in sent]
    core_own = other_core(occ)

    origin = [place, place ^ 1]
    for by in shifts:
        origin += [(place - by) % n_cls, ((place ^ 1) - by) % n_cls]
    mine = jnp.concatenate(
        [lax.dynamic_slice_in_dim(r, place * rows, rows, axis=1) for r in (stay_rows[0], rise_rows[0])], axis=1
    ).T
    mine = jnp.concatenate([lax.dynamic_slice_in_dim(mine, o * rows, rows, axis=1) for o in origin], axis=1)
    a_hi, a_lo = halves_outside(mine)
    a_both = jnp.concatenate([a_hi, a_lo], axis=0)

    base, rise = local_terms(
        occ,
        lax.dynamic_slice_in_dim(out_rows[0], place * rows, rows),
        jnp.concatenate([stay_rows[2], rise_rows[2]], axis=1),
        jnp.concatenate([stay_rows[1], rise_rows[1]], axis=1).T,
        out_rows[1][:, None],
        (uniform_rate - out_rows[2] - drop_here)[None, :],
    )

    scale = (1.0 / uniform_rate)[None]
    out = None
    for k, (at, size) in enumerate(chunks):
        slabs = [(occ, at), (core_own, at)]
        for v in far[k]:
            slabs += [(v, 0), (other_core(v), 0)]
        stay_k, rise_k = first_terms(a_both, a_hi, slabs, base, rise, at, size)
        lifted = two_up(rise_k)
        send = jnp.where(even, rise_k, lifted) + once_deep * deep[k] + once_here * sent[k]
        risen = pair_swap(send)
        out = finish(out, occ.shape, scale, stay_k, twice_deep, risen, deep[k], at, size)
    return out[None]


def solution(mesh):
    in_specs = (P("lvl", "cls", None, None), P(), P(), P(), P(), P())
    out_specs = P("lvl", "cls", None, None)
    return jax.shard_map(local, mesh=mesh, in_specs=in_specs, out_specs=out_specs, check_vma=False)
```

```python
import functools

import jax
import jax.numpy as jnp
from jax import lax
from jax.experimental import pallas as pl
from jax.experimental.pallas import tpu as pltpu
from jax.sharding import PartitionSpec as P

F32 = jnp.float32
BF16 = jnp.bfloat16
VMEM_LIMIT = 56 * 2**20
SPAN, LANES = 8, 128
LIGHT = pl.CostEstimate(flops=1000, transcendentals=0, bytes_accessed=1000)
PARAMS = pltpu.CompilerParams(vmem_limit_bytes=VMEM_LIMIT)
WHOLE = pl.BlockSpec(memory_space=pltpu.VMEM)


def gate(*values):
    return lax.optimization_barrier(values)


def flag(cond):
    return jnp.where(cond, 1.0, 0.0).astype(F32)


def halves(x):
    high = x.astype(BF16)
    low = (x - high.astype(F32)).astype(BF16)
    return high, low


def halves_outside(x):
    high = lax.reduce_precision(x, 8, 7)
    return high.astype(BF16), (x - high).astype(BF16)


def dot(a, b):
    return jnp.dot(a, b, preferred_element_type=F32)


def chunk_bounds(length):
    sizes = [1, 1, 2, 2, 2, 2, 2, 2, 1, 1]
    unit = length // sum(sizes)
    bounds, at = [], 0
    for size in sizes:
        bounds.append((at, size * unit))
        at += size * unit
    return bounds


def local_kernel(at, half, core, own_rows, occ, c_hi, c_lo, b_hi, b_lo, row_b, row_c, mine, peer):
    block, phases = occ.shape[0], occ.shape[2]
    size = mine.shape[2]
    first = pl.program_id(0) * block
    rows = [pl.ds(pl.multiple_of(core[n] * half + at, SPAN), size) for n in range(2)]
    for i in range(block):
        x = occ[i]
        x_hi, x_lo = halves(x)
        by_b = dot(b_hi[...], x_hi) + dot(b_hi[...], x_lo) + dot(b_lo[...], x_hi)
        y = jnp.concatenate([occ[i, rows[0]], occ[i, rows[1]]], axis=0)
        y_hi, y_lo = halves(y)
        by_c = dot(y_hi, c_hi[...]) + dot(y_lo, c_hi[...]) + dot(y_hi, c_lo[...])
        left = row_c[...] - own_rows[first + i] - row_b[...]
        base = by_c[:, :phases] + by_b[: 2 * size] + y * left
        rise = by_c[:, phases:] + by_b[2 * size :]
        mine[0, i] = base[:size]
        peer[0, i] = base[size:]
        mine[1, i] = rise[:size]
        peer[1, i] = rise[size:]


def local_terms(core, occ, own_rows, c_split, b_split, row_b, row_c, at, size):
    rows, mid, phases = occ.shape
    block = 4
    out = pl.BlockSpec((2, block, size, phases), lambda i, c: (0, i, 0, 0))
    return pl.pallas_call(
        functools.partial(local_kernel, at, mid // 2),
        grid_spec=pltpu.PrefetchScalarGridSpec(
            num_scalar_prefetch=1,
            grid=(rows // block,),
            in_specs=[
                pl.BlockSpec(memory_space=pltpu.SMEM),
                pl.BlockSpec((block, mid, phases), lambda i, c: (i, 0, 0)),
            ]
            + [WHOLE] * 6,
            out_specs=[out, out],
        ),
        out_shape=[jax.ShapeDtypeStruct((2, rows, size, phases), F32)] * 2,
        compiler_params=PARAMS,
        cost_estimate=LIGHT,
        name="local_terms",
    )(core, own_rows, occ, *c_split, *b_split, row_b, row_c)


def first_kernel(n_slabs, *refs):
    w_both, w_hi = refs[0], refs[1]
    slabs = refs[2 : 2 + n_slabs]
    mine, peer, stay_out, rise_out = refs[2 + n_slabs :]
    rows, span, lanes = stay_out.shape
    flat = [ref.reshape(rows * span, lanes) for ref in slabs]
    stay_flat = stay_out.reshape(rows * span, lanes)
    rise_flat = rise_out.reshape(rows * span, lanes)
    for b in range(0, span, 2):
        ats = [pl.ds(b, rows, stride=span), pl.ds(b + 1, rows, stride=span)]
        parts = [halves(jnp.concatenate([ref[at, :] for at in ats], axis=1)) for ref in flat]
        g_hi = jnp.concatenate([p[0] for p in parts], axis=0)
        g_lo = jnp.concatenate([p[1] for p in parts], axis=0)
        both = dot(w_both[...], g_hi)
        out = both[: 2 * rows] + both[2 * rows :] + dot(w_hi[...], g_lo)
        for n, at in enumerate(ats):
            stay_flat[at, :] = out[:rows, n * lanes : (n + 1) * lanes]
            rise_flat[at, :] = out[rows:, n * lanes : (n + 1) * lanes]
    half = rows // 2
    stay_out[:half] += mine[0]
    stay_out[half:] += peer[0]
    rise_out[:half] += mine[1]
    rise_out[half:] += peer[1]


def first_terms(w_both, w_hi, slabs, mine, peer, start):
    rows, size, phases = slabs[0].shape
    chunk = pl.BlockSpec((rows, SPAN, LANES), lambda j, h: (0, j, h))
    local_part = pl.BlockSpec((2, rows // 2, SPAN, LANES), lambda j, h: (0, 0, start // SPAN + j, h))
    return pl.pallas_call(
        functools.partial(first_kernel, len(slabs)),
        grid=(size // SPAN, phases // LANES),
        in_specs=[WHOLE, WHOLE] + [chunk] * len(slabs) + [local_part] * 2,
        out_specs=[chunk, chunk],
        out_shape=[jax.ShapeDtypeStruct((rows, size, phases), F32)] * 2,
        compiler_params=PARAMS,
        cost_estimate=LIGHT,
        name="first_terms",
    )(w_both, w_hi, *slabs, mine, peer)


def turn_kernel(parity, rise, lifted, deep, here, fall, out):
    @pl.when(parity[0] == 0)
    def _():
        out[...] = rise[...] + fall[1:2] * deep[...]

    @pl.when(parity[0] != 0)
    def _():
        out[...] = lifted[...] + fall[0:1] * here[...]


def turn(parity, rise, lifted, deep, here, fall):
    rows, size, phases = rise.shape
    chunk = pl.BlockSpec((rows, SPAN, phases), lambda j: (0, j, 0))
    return pl.pallas_call(
        turn_kernel,
        grid=(size // SPAN,),
        in_specs=[pl.BlockSpec(memory_space=pltpu.SMEM)] + [chunk] * 4 + [WHOLE],
        out_specs=chunk,
        out_shape=jax.ShapeDtypeStruct(rise.shape, F32),
        compiler_params=PARAMS,
        cost_estimate=LIGHT,
        name="turn",
    )(parity, rise, lifted, deep, here, fall)


def finish_kernel(has_out, core, scale, stay, fall, risen, deep, *refs):
    out, back = refs[has_out:]
    value = (stay[...] + risen[...] + fall[2:3] * deep[...]) * scale[0]
    half = value.shape[0] // 2
    out[...] = value[:half]
    back[...] = value[half:]


def finish(core, out, shape, scale, stay, fall, risen, deep, start):
    rows, size, phases = stay.shape
    chunk = pl.BlockSpec((rows, SPAN, phases), lambda j, c: (0, j, 0))
    steps = shape[1] // 2 // SPAN
    args = [core, scale, stay, fall, risen, deep]
    specs = [pl.BlockSpec(memory_space=pltpu.SMEM), chunk, WHOLE, chunk, chunk]
    alias = {}
    if out is not None:
        alias = {len(args): 0}
        args.append(out)
        specs.append(pl.BlockSpec(memory_space=pl.ANY))
    return pl.pallas_call(
        functools.partial(finish_kernel, len(alias)),
        grid_spec=pltpu.PrefetchScalarGridSpec(
            num_scalar_prefetch=1,
            grid=(size // SPAN,),
            in_specs=specs,
            out_specs=[
                pl.BlockSpec((rows // 2, SPAN, phases), lambda j, c: (0, c[0] * steps + start // SPAN + j, 0)),
                pl.BlockSpec((rows // 2, SPAN, phases), lambda j, c: (0, j, 0)),
            ],
        ),
        out_shape=[jax.ShapeDtypeStruct(shape, F32), jax.ShapeDtypeStruct((rows // 2, size, phases), F32)],
        input_output_aliases=alias,
        compiler_params=PARAMS,
        cost_estimate=LIGHT,
        name="finish",
    )(*args)


def place_kernel(core, piece, _, out):
    out[...] = piece[...]


def put(core, out, piece, start):
    rows, size, phases = piece.shape
    steps = out.shape[1] // 2 // SPAN
    return pl.pallas_call(
        place_kernel,
        grid_spec=pltpu.PrefetchScalarGridSpec(
            num_scalar_prefetch=1,
            grid=(size // SPAN,),
            in_specs=[
                pl.BlockSpec((rows, SPAN, phases), lambda j, c: (0, j, 0)),
                pl.BlockSpec(memory_space=pl.ANY),
            ],
            out_specs=pl.BlockSpec((rows, SPAN, phases), lambda j, c: (0, c[1] * steps + start // SPAN + j, 0)),
        ),
        out_shape=jax.ShapeDtypeStruct(out.shape, F32),
        input_output_aliases={2: 0},
        compiler_params=PARAMS,
        cost_estimate=LIGHT,
        name="put",
    )(core, piece, out)


def local(occupancy, rates, increments, draw, crusher_rate, bounds):
    n_cls, n_lvl = lax.axis_size("cls"), lax.axis_size("lvl")
    occ = occupancy[0]
    rows, mid, phases = occ.shape
    half = mid // 2
    level = lax.axis_index("lvl")
    place = lax.axis_index("cls")
    k = place % 2
    core = jnp.stack([k, 1 - k])
    even = level % 2 == 0
    bottom, top = bounds[0], bounds[1]

    def along_cls(v, by):
        return lax.ppermute(v, "cls", [(i, (i + by) % n_cls) for i in range(n_cls)])

    def other_core(v):
        return lax.ppermute(v, "cls", [(i, i ^ 1) for i in range(n_cls)])

    def two_down(v):
        return lax.ppermute(v, "lvl", [(i, i - 2) for i in range(2, n_lvl)])

    def two_up(v):
        return lax.ppermute(v, "lvl", [(i, i + 2) for i in range(1, n_lvl - 2, 2)])

    def pair_swap(v):
        return lax.ppermute(v, "lvl", [(i, i ^ 1) for i in range(n_lvl)])

    def cut(array, which, at, size):
        return lax.dynamic_slice_in_dim(array, core[which] * half + at, size, axis=1)

    chunks = chunk_bounds(half)
    n = len(chunks)
    shifts = [2 * s for s in range(1, n_cls // 2)]
    pieces = [(0, 1), (1, 3), (3, n)]
    sent = [None] * n
    token, tokens = None, []
    for lo, hi in pieces:
        at = chunks[lo][0]
        size = chunks[hi - 1][0] + chunks[hi - 1][1] - at
        give = cut(occ, 1, at, size)
        if token is not None:
            give, _ = gate(give, token)
        token = got = other_core(give)
        tokens.append(got)
        for s in range(lo, hi):
            start, length = chunks[s]
            own = cut(occ, 0, start, length)
            sent[s] = jnp.concatenate([own, lax.slice_in_dim(got, start - at, start - at + length, axis=1)], axis=0)

    far, deep = [None] * n, [None] * n

    def start_far(s, *after):
        operand = gate(sent[s], *after)[0] if after else sent[s]
        far[s] = [along_cls(operand, by) for by in shifts]

    def start_deep(s, *after):
        operand = gate(sent[s], *after)[0] if after else sent[s]
        deep[s] = two_down(operand)

    start_far(0)
    start_far(1)
    start_deep(0)

    row_total = jnp.sum(rates, axis=2)
    uniform_rate = jnp.sum(jnp.max(row_total, axis=1)) + jnp.max(crusher_rate)
    out_rows = row_total * flag((increments == 0) | (level + increments <= top))
    rise_ok = flag(level + 1 <= top)
    drop_here = crusher_rate * flag(level - draw >= bottom)
    drop_deep = crusher_rate * flag(level + 2 - draw >= bottom)
    once_here = (drop_here * flag(draw == 1) * flag(~even))[None, :]
    once_deep = (drop_deep * flag(draw == 1) * flag(even))[None, :]
    twice_deep = (drop_deep * flag(draw == 2))[None, :]
    fall_vec = jnp.concatenate([once_here, once_deep, twice_deep], axis=0)
    parity = (level % 2)[None]
    scale = (1.0 / uniform_rate)[None]

    stay_rows = rates * flag(increments == 0)[:, :, None]
    rise_rows = rates * (flag(increments == 1) * rise_ok)[:, :, None]

    c_split = halves_outside(jnp.concatenate([stay_rows[2], rise_rows[2]], axis=1))
    own_rows = lax.dynamic_slice_in_dim(out_rows[0], place * rows, rows)
    row_c = (uniform_rate - out_rows[2] - drop_here)[None, :]
    cuts = [(0, 2), (2, n)]
    parts = []
    for lo, hi in cuts:
        at = chunks[lo][0]
        size = chunks[hi - 1][0] + chunks[hi - 1][1] - at
        cat_b = jnp.concatenate([cut(r, w, at, size) for r in (stay_rows[1], rise_rows[1]) for w in range(2)], axis=1)
        row_b = jnp.concatenate([lax.dynamic_slice_in_dim(out_rows[1], core[w] * half + at, size) for w in range(2)])
        here = gate(occ, tokens[len(parts)], *(p[3] for p in parts))[0]
        mine, give = local_terms(
            core, here, own_rows, c_split, halves_outside(cat_b.T), row_b[:, None], row_c, at, size
        )
        parts += [(lo, hi, at, mine, other_core(give))]

    origin = [place, place ^ 1]
    for by in shifts:
        origin += [(place - by) % n_cls, ((place - by) % n_cls) ^ 1]
    mine = jnp.concatenate(
        [
            lax.dynamic_slice_in_dim(r, p * rows, rows, axis=1)
            for r in (stay_rows[0], rise_rows[0])
            for p in (place, place ^ 1)
        ],
        axis=1,
    ).T
    mine = jnp.concatenate([lax.dynamic_slice_in_dim(mine, o * rows, rows, axis=1) for o in origin], axis=1)
    a_hi, a_lo = halves_outside(mine)
    a_both = jnp.concatenate([a_hi, a_lo], axis=0)

    out = None
    stay, rise, lifted, risen, back = ([None] * n for _ in range(5))

    def close(s):
        return finish(core, out, occ.shape, scale, stay[s], fall_vec, risen[s], deep[s], chunks[s][0])

    for s in range(n + 3):
        if s < n:
            if s >= 3:
                far[s][0], risen[s - 3] = gate(far[s][0], risen[s - 3])
            if s >= 4:
                far[s][0], out = gate(far[s][0], out)
            if s + 2 < n:
                start_far(s + 2, far[s][0])
            if s + 1 < n:
                start_deep(s + 1, far[s][0], deep[s])
            lo, hi, at, mine, peer = next(p for p in parts if p[0] <= s < p[1])
            stay[s], rise[s] = first_terms(a_both, a_hi, [sent[s]] + far[s], mine, peer, chunks[s][0] - at)
            lift_me = rise[s]
            if s >= 1:
                lift_me, lifted[s - 1] = gate(lift_me, lifted[s - 1])
            lifted[s] = two_up(lift_me)
        if 1 <= s <= n:
            p = s - 1
            swap_me = turn(parity, rise[p], lifted[p], deep[p], sent[p], fall_vec)
            if p >= 1:
                swap_me, risen[p - 1] = gate(swap_me, risen[p - 1])
            risen[p] = pair_swap(swap_me)
        if 0 <= s - 2 < n:
            out, give = close(s - 2)
            back[s - 2] = other_core(give)
        if 0 <= s - 3 < n:
            out = put(core, out, back[s - 3], chunks[s - 3][0])
    return out[None]


def solution(mesh):
    in_specs = (P("lvl", "cls", None, None), P(), P(), P(), P(), P())
    out_specs = P("lvl", "cls", None, None)
    return jax.shard_map(local, mesh=mesh, in_specs=in_specs, out_specs=out_specs, check_vma=False)
```

```python
import functools

import jax
import jax.numpy as jnp
from jax import lax
from jax.experimental import pallas as pl
from jax.experimental.pallas import tpu as pltpu
from jax.sharding import PartitionSpec as P

F32 = jnp.float32
BF16 = jnp.bfloat16
VMEM_LIMIT = 56 * 2**20
SPAN, LANES = 8, 128
LIGHT = pl.CostEstimate(flops=1000, transcendentals=0, bytes_accessed=1000)
PARAMS = pltpu.CompilerParams(vmem_limit_bytes=VMEM_LIMIT)
WHOLE = pl.BlockSpec(memory_space=pltpu.VMEM)


def gate(*values):
    return lax.optimization_barrier(values)


def flag(cond):
    return jnp.where(cond, 1.0, 0.0).astype(F32)


def halves(x):
    high = x.astype(BF16)
    low = (x - high.astype(F32)).astype(BF16)
    return high, low


def halves_outside(x):
    high = lax.reduce_precision(x, 8, 7)
    return high.astype(BF16), (x - high).astype(BF16)


def dot(a, b):
    return jnp.dot(a, b, preferred_element_type=F32)


def plan(rows, length):
    n = max(4, min(length // SPAN, rows // 4))
    size = length // n
    chunks = [(s * size, size) for s in range(n)]
    groups, at = [], 0
    while at < n:
        step = 4 if n - at > 4 else max(1, (n - at) // 2)
        groups.append((at, at + step))
        at += step
    return chunks, groups


def spans(*bounds):
    return list(zip(bounds[:-1], bounds[1:]))


def local_kernel(at, half, core, own_rows, occ, c_hi, c_lo, b_hi, b_lo, row_b, row_c, *outs):
    block, phases = occ.shape[0], occ.shape[2]
    size = outs[0].shape[1]
    first = pl.program_id(0) * block
    rows = [pl.ds(pl.multiple_of(core[n] * half + at, SPAN), size) for n in range(2)]
    y = jnp.concatenate([occ[i, r] for i in range(block) for r in rows], axis=0)
    y_hi, y_lo = halves(y)
    by_c = dot(y_hi, c_hi[...]) + dot(y_lo, c_hi[...]) + dot(y_hi, c_lo[...])
    for i in range(block):
        x_hi, x_lo = halves(occ[i])
        by_b = dot(b_hi[...], x_hi) + dot(b_hi[...], x_lo) + dot(b_lo[...], x_hi)
        here = slice(2 * size * i, 2 * size * (i + 1))
        left = row_c[...] - own_rows[first + i] - row_b[...]
        base = by_c[here, :phases] + by_b[: 2 * size] + y[here] * left
        rise = by_c[here, phases:] + by_b[2 * size :]
        for n, value in enumerate((base, rise)):
            outs[n][i] = value[:size]
            outs[n + 2][i] = value[size:]


def local_terms(core, occ, own_rows, c_split, b_split, row_b, row_c, at, size):
    rows, mid, phases = occ.shape
    block = 4
    out = pl.BlockSpec((block, size, phases), lambda i, c: (i, 0, 0))
    return pl.pallas_call(
        functools.partial(local_kernel, at, mid // 2),
        grid_spec=pltpu.PrefetchScalarGridSpec(
            num_scalar_prefetch=1,
            grid=(rows // block,),
            in_specs=[
                pl.BlockSpec(memory_space=pltpu.SMEM),
                pl.BlockSpec((block, mid, phases), lambda i, c: (i, 0, 0)),
            ]
            + [WHOLE] * 6,
            out_specs=[out] * 4,
        ),
        out_shape=[jax.ShapeDtypeStruct((rows, size, phases), F32)] * 4,
        compiler_params=PARAMS,
        cost_estimate=LIGHT,
        name="local_terms",
    )(core, own_rows, occ, *c_split, *b_split, row_b, row_c)


def first_kernel(n_slabs, *refs):
    w_both, w_hi = refs[0], refs[1]
    slabs = refs[2 : 2 + n_slabs]
    mine_base, mine_rise, peer_base, peer_rise, stay_out, rise_out = refs[2 + n_slabs :]
    rows, span, lanes = stay_out.shape
    flat = [ref.reshape(ref.shape[0] * span, lanes) for ref in slabs]
    stay_flat = stay_out.reshape(rows * span, lanes)
    rise_flat = rise_out.reshape(rows * span, lanes)
    for b in range(0, span, 2):
        ats = [pl.ds(b, rows, stride=span), pl.ds(b + 1, rows, stride=span)]
        parts = []
        for ref in flat:
            picks = [pl.ds(b + n, ref.shape[0] // span, stride=span) for n in range(2)]
            parts.append(halves(jnp.concatenate([ref[pick, :] for pick in picks], axis=1)))
        g_hi = jnp.concatenate([p[0] for p in parts], axis=0)
        g_lo = jnp.concatenate([p[1] for p in parts], axis=0)
        both = dot(w_both[...], g_hi)
        out = both[: 2 * rows] + both[2 * rows :] + dot(w_hi[...], g_lo)
        for n, at in enumerate(ats):
            stay_flat[at, :] = out[:rows, n * lanes : (n + 1) * lanes]
            rise_flat[at, :] = out[rows:, n * lanes : (n + 1) * lanes]
    half = rows // 2
    stay_out[:half] += mine_base[...]
    stay_out[half:] += peer_base[...]
    rise_out[:half] += mine_rise[...]
    rise_out[half:] += peer_rise[...]


def first_terms(w_both, w_hi, slabs, near, start):
    rows, size, phases = slabs[0].shape
    slab_specs = [pl.BlockSpec((v.shape[0], SPAN, LANES), lambda j, h: (0, j, h)) for v in slabs]
    chunk = pl.BlockSpec((rows, SPAN, LANES), lambda j, h: (0, j, h))
    local_part = pl.BlockSpec((rows // 2, SPAN, LANES), lambda j, h: (0, start // SPAN + j, h))
    return pl.pallas_call(
        functools.partial(first_kernel, len(slabs)),
        grid=(size // SPAN, phases // LANES),
        in_specs=[WHOLE, WHOLE] + slab_specs + [local_part] * 4,
        out_specs=[chunk, chunk],
        out_shape=[jax.ShapeDtypeStruct((rows, size, phases), F32)] * 2,
        compiler_params=PARAMS,
        cost_estimate=LIGHT,
        name="first_terms",
    )(w_both, w_hi, *slabs, *near)


def turn_kernel(parity, rise, lifted, deep, here, fall, out):
    @pl.when(parity[0] == 0)
    def _():
        out[...] = rise[...] + fall[1:2] * deep[...]

    @pl.when(parity[0] != 0)
    def _():
        out[...] = lifted[...] + fall[0:1] * here[...]


def turn(parity, rise, lifted, deep, deep_at, here, fall):
    rows, size, phases = rise.shape
    block = min(32, rows)
    chunk = pl.BlockSpec((block, SPAN, phases), lambda i, j: (i, j, 0))
    deep_chunk = pl.BlockSpec((block, SPAN, phases), lambda i, j: (i, deep_at // SPAN + j, 0))
    return pl.pallas_call(
        turn_kernel,
        grid=(rows // block, size // SPAN),
        in_specs=[pl.BlockSpec(memory_space=pltpu.SMEM), chunk, chunk, deep_chunk, chunk, WHOLE],
        out_specs=chunk,
        out_shape=jax.ShapeDtypeStruct(rise.shape, F32),
        compiler_params=PARAMS,
        cost_estimate=LIGHT,
        name="turn",
    )(parity, rise, lifted, deep, here, fall)


def finish_kernel(n_alias, core, scale, fall, *refs):
    out, back = refs[6 + n_alias :]
    for n, target in enumerate((out, back)):
        stay, risen, deep = refs[n], refs[2 + n], refs[4 + n]
        target[...] = (stay[...] + risen[...] + fall[2:3] * deep[...]) * scale[0]


def finish(core, out, back, shape, back_size, scale, stay, fall, risen, deep, deep_at, start, back_at):
    rows, size, phases = stay.shape
    block = min(32, rows // 2)
    blocks = rows // 2 // block
    steps = shape[1] // 2 // SPAN

    def part(offset, which):
        return pl.BlockSpec((block, SPAN, phases), lambda i, j, c: (which * blocks + i, offset // SPAN + j, 0))

    args = [core, scale, fall]
    specs = [pl.BlockSpec(memory_space=pltpu.SMEM), WHOLE]
    for array, offset in ((stay, 0), (risen, 0), (deep, deep_at)):
        args += [array, array]
        specs += [part(offset, 0), part(offset, 1)]
    alias = {}
    for n, old in enumerate((out, back)):
        if old is not None:
            alias[len(args)] = n
            args.append(old)
            specs.append(pl.BlockSpec(memory_space=pl.ANY))
    return pl.pallas_call(
        functools.partial(finish_kernel, len(alias)),
        grid_spec=pltpu.PrefetchScalarGridSpec(
            num_scalar_prefetch=1,
            grid=(blocks, size // SPAN),
            in_specs=specs,
            out_specs=[
                pl.BlockSpec((block, SPAN, phases), lambda i, j, c: (i, c[0] * steps + start // SPAN + j, 0)),
                pl.BlockSpec((block, SPAN, phases), lambda i, j, c: (i, back_at // SPAN + j, 0)),
            ],
        ),
        out_shape=[jax.ShapeDtypeStruct(shape, F32), jax.ShapeDtypeStruct((rows // 2, back_size, phases), F32)],
        input_output_aliases=alias,
        compiler_params=PARAMS,
        cost_estimate=LIGHT,
        name="finish",
    )(*args)


def put_kernel(core, piece, _, out):
    out[...] = piece[...]


def put(core, out, piece, start):
    rows, size, phases = piece.shape
    block = min(16, rows)
    steps = out.shape[1] // 2 // SPAN
    return pl.pallas_call(
        put_kernel,
        grid_spec=pltpu.PrefetchScalarGridSpec(
            num_scalar_prefetch=1,
            grid=(rows // block, size // SPAN),
            in_specs=[
                pl.BlockSpec((block, SPAN, phases), lambda i, j, c: (i, j, 0)),
                pl.BlockSpec(memory_space=pl.ANY),
            ],
            out_specs=pl.BlockSpec((block, SPAN, phases), lambda i, j, c: (i, c[1] * steps + start // SPAN + j, 0)),
        ),
        out_shape=jax.ShapeDtypeStruct(out.shape, F32),
        input_output_aliases={2: 0},
        compiler_params=PARAMS,
        cost_estimate=LIGHT,
        name="put",
    )(core, piece, out)


def local(occupancy, rates, increments, draw, crusher_rate, bounds):
    n_cls, n_lvl = lax.axis_size("cls"), lax.axis_size("lvl")
    occ = occupancy[0]
    rows, mid, phases = occ.shape
    half = mid // 2
    level = lax.axis_index("lvl")
    place = lax.axis_index("cls")
    k = place % 2
    core = jnp.stack([k, 1 - k])
    even = level % 2 == 0
    bottom, top = bounds[0], bounds[1]

    def along_cls(v, by):
        return lax.ppermute(v, "cls", [(i, (i + by) % n_cls) for i in range(n_cls)])

    def other_core(v):
        return lax.ppermute(v, "cls", [(i, i ^ 1) for i in range(n_cls)])

    def two_down(v):
        return lax.ppermute(v, "lvl", [(i, i - 2) for i in range(2, n_lvl)])

    def two_up(v):
        return lax.ppermute(v, "lvl", [(i, i + 2) for i in range(1, n_lvl - 2, 2)])

    def pair_swap(v):
        return lax.ppermute(v, "lvl", [(i, i ^ 1) for i in range(n_lvl)])

    def cut(array, which, at, size):
        return lax.dynamic_slice_in_dim(array, core[which] * half + at, size, axis=1)

    chunks, groups = plan(rows, half)
    n = len(chunks)
    size = chunks[0][1]
    shifts = [2 * s for s in range(1, n_cls // 2)]
    sent = [None] * n
    tokens = []
    for lo, hi in spans(*sorted({0, 1, 4, n})):
        at = chunks[lo][0]
        give = cut(occ, 1, at, (hi - lo) * size)
        if tokens:
            give, _ = gate(give, tokens[-1])
        got = other_core(give)
        tokens.append(got)
        for s in range(lo, hi):
            start = chunks[s][0]
            part = lax.slice_in_dim(got, start - at, start - at + size, axis=1)
            sent[s] = jnp.concatenate([cut(occ, 0, start, size), part], axis=0)

    far, deep = [None] * n, [None] * n

    def start_early(s):
        for by in shifts:
            straight = along_cls(cut(occ, 0, s * size, size), by)
            crossed = [(i, ((i + by) % n_cls) ^ 1) for i in range(n_cls)]
            cross = lax.ppermute(cut(occ, 1, s * size, size), "cls", crossed)
            far[s] = (far[s] or []) + [straight, cross]

    def start_far(s, *after):
        operand = gate(sent[s], *after)[0] if after else sent[s]
        far[s] = [along_cls(operand, by) for by in shifts]

    def start_deep(s, *after):
        operand = jnp.concatenate([sent[s], sent[s + 1]], axis=1)
        if after:
            operand = gate(operand, *after)[0]
        got = two_down(operand)
        deep[s], deep[s + 1] = (got, 0), (got, size)

    start_early(0)
    start_early(1)
    start_deep(0)

    row_total = jnp.sum(rates, axis=2)
    uniform_rate = jnp.sum(jnp.max(row_total, axis=1)) + jnp.max(crusher_rate)
    out_rows = row_total * flag((increments == 0) | (level + increments <= top))
    rise_ok = flag(level + 1 <= top)
    drop_here = crusher_rate * flag(level - draw >= bottom)
    drop_deep = crusher_rate * flag(level + 2 - draw >= bottom)
    once_here = (drop_here * flag(draw == 1) * flag(~even))[None, :]
    once_deep = (drop_deep * flag(draw == 1) * flag(even))[None, :]
    twice_deep = (drop_deep * flag(draw == 2))[None, :]
    fall_vec = jnp.concatenate([once_here, once_deep, twice_deep], axis=0)
    parity = (level % 2)[None]
    scale = (1.0 / uniform_rate)[None]

    stay_rows = rates * flag(increments == 0)[:, :, None]
    rise_rows = rates * (flag(increments == 1) * rise_ok)[:, :, None]

    c_split = halves_outside(jnp.concatenate([stay_rows[2], rise_rows[2]], axis=1))
    own_rows = lax.dynamic_slice_in_dim(out_rows[0], place * rows, rows)
    row_c = (uniform_rate - out_rows[2] - drop_here)[None, :]
    parts = []

    def start_part(lo, hi, *after):
        at, span = chunks[lo][0], (hi - lo) * size
        cat_b = jnp.concatenate([cut(r, w, at, span) for r in (stay_rows[1], rise_rows[1]) for w in range(2)], axis=1)
        row_b = jnp.concatenate([lax.dynamic_slice_in_dim(out_rows[1], core[w] * half + at, span) for w in range(2)])
        base, rise, give_base, give_rise = local_terms(
            core, gate(occ, *after)[0], own_rows, c_split, halves_outside(cat_b.T), row_b[:, None], row_c, at, span
        )
        parts.append((lo, hi, at, (base, rise, other_core(give_base), other_core(give_rise))))
        return base

    local_spans = spans(*sorted({0, 1, n // 4, n // 2, n}))
    token = start_part(*local_spans[0], tokens[0])
    token = start_part(*local_spans[1], token)
    far[0][0], _ = gate(far[0][0], token)

    origin = [place, place ^ 1]
    for by in shifts:
        origin += [(place - by) % n_cls, ((place - by) % n_cls) ^ 1]
    mine = jnp.concatenate(
        [
            lax.dynamic_slice_in_dim(r, p * rows, rows, axis=1)
            for r in (stay_rows[0], rise_rows[0])
            for p in (place, place ^ 1)
        ],
        axis=1,
    ).T
    mine = jnp.concatenate([lax.dynamic_slice_in_dim(mine, o * rows, rows, axis=1) for o in origin], axis=1)
    a_hi, a_lo = halves_outside(mine)
    a_both = jnp.concatenate([a_hi, a_lo], axis=0)

    out = None
    stay, rise, lifted, risen = ([None] * n for _ in range(4))
    back = [None] * len(groups)
    group_of = {s: g for g, (lo, hi) in enumerate(groups) for s in range(lo, hi)}

    for s in range(n + 4):
        if s < n:
            if s >= 3:
                far[s][0], risen[s - 3] = gate(far[s][0], risen[s - 3])
            if s >= 4:
                far[s][0], out = gate(far[s][0], out)
            if s + 2 < n:
                start_far(s + 2, far[s][0])
            if s % 2 and s + 1 < n:
                start_deep(s + 1, far[s][0], deep[s][0])
            lo, hi, at, near = next(p for p in parts if p[0] <= s < p[1])
            stay[s], rise[s] = first_terms(a_both, a_hi, [sent[s]] + far[s], near, chunks[s][0] - at)
            if s + 1 in (lo for lo, _ in local_spans[2:]):
                start_part(*next(v for v in local_spans if v[0] == s + 1), rise[max(0, s - 2)])
            lift_me = rise[s]
            if s >= 1:
                lift_me, lifted[s - 1] = gate(lift_me, lifted[s - 1])
            lifted[s] = two_up(lift_me)
        if 1 <= s <= n:
            p = s - 1
            swap_me = turn(parity, rise[p], lifted[p], *deep[p], sent[p], fall_vec)
            if p >= 1:
                swap_me, risen[p - 1] = gate(swap_me, risen[p - 1])
            risen[p] = pair_swap(swap_me)
        if 0 <= s - 2 < n:
            p = s - 2
            g = group_of[p]
            lo, hi = groups[g]
            out, back[g] = finish(
                core, out, back[g], occ.shape, (hi - lo) * size, scale, stay[p], fall_vec, risen[p], *deep[p],
                chunks[p][0], (p - lo) * size,
            )
            if p == hi - 1:
                back[g] = other_core(back[g])
        if 0 <= s - 3 < n:
            p = s - 3
            lo, hi = groups[group_of[p]]
            if p == hi - 1:
                out = put(core, out, back[group_of[p]], chunks[lo][0])
    return out[None]


def solution(mesh):
    in_specs = (P("lvl", "cls", None, None), P(), P(), P(), P(), P())
    out_specs = P("lvl", "cls", None, None)
    return jax.shard_map(local, mesh=mesh, in_specs=in_specs, out_specs=out_specs, check_vma=False)
```

```python
import functools

import jax
import jax.numpy as jnp
from jax import lax
from jax.experimental import pallas as pl
from jax.experimental.pallas import tpu as pltpu
from jax.sharding import PartitionSpec as P

F32 = jnp.float32
BF16 = jnp.bfloat16
VMEM_LIMIT = 56 * 2**20
SPAN, LANES = 8, 128
LIGHT = pl.CostEstimate(flops=1000, transcendentals=0, bytes_accessed=1000)
PARAMS = pltpu.CompilerParams(vmem_limit_bytes=VMEM_LIMIT)
WHOLE = pl.BlockSpec(memory_space=pltpu.VMEM)


def gate(*values):
    return lax.optimization_barrier(values)


def flag(cond):
    return jnp.where(cond, 1.0, 0.0).astype(F32)


def halves(x):
    high = x.astype(BF16)
    low = (x - high.astype(F32)).astype(BF16)
    return high, low


def halves_outside(x):
    high = lax.reduce_precision(x, 8, 7)
    return high.astype(BF16), (x - high).astype(BF16)


def dot(a, b):
    return jnp.dot(a, b, preferred_element_type=F32)


def plan(rows, length):
    n = max(4, min(length // SPAN, rows // 4))
    size = length // n
    chunks = [(s * size, size) for s in range(n)]
    groups, at = [], 0
    while at < n:
        step = 4 if n - at > 4 else max(1, (n - at) // 2)
        groups.append((at, at + step))
        at += step
    return chunks, groups


def spans(*bounds):
    return list(zip(bounds[:-1], bounds[1:]))


def local_kernel(at, half, core, own_rows, occ, c_hi, c_lo, b_both, row_b, row_c, *outs):
    block, phases = occ.shape[0], occ.shape[2]
    size = outs[0].shape[2]
    first = pl.program_id(0) * block
    rows = [pl.ds(pl.multiple_of(core[n] * half + at, SPAN), size) for n in range(2)]
    y = jnp.concatenate([occ[i, r] for i in range(block) for r in rows], axis=0)
    y_hi, y_lo = halves(y)
    n_y = y.shape[0]
    by_c = dot(jnp.concatenate([y_hi, y_lo], axis=0), c_hi[...])
    by_c = by_c[:n_y] + by_c[n_y:] + dot(y_hi, c_lo[...])
    for i in range(block):
        x_hi, x_lo = halves(occ[i])
        by_b = dot(b_both[...], x_hi)
        by_b = by_b[: 4 * size] + by_b[4 * size :] + dot(b_both[: 4 * size], x_lo)
        here = slice(2 * size * i, 2 * size * (i + 1))
        left = row_c[...] - own_rows[first + i] - row_b[...]
        base = by_c[here, :phases] + by_b[: 2 * size] + y[here] * left
        rise = by_c[here, phases:] + by_b[2 * size :]
        mine, peer = outs
        for n, value in enumerate((base, rise)):
            mine[n, i] = value[:size]
            peer[n, i] = value[size:]


def local_terms(core, occ, own_rows, c_split, b_both, row_b, row_c, at, size):
    rows, mid, phases = occ.shape
    block = 8
    out = pl.BlockSpec((2, block, size, phases), lambda i, c: (0, i, 0, 0))
    return pl.pallas_call(
        functools.partial(local_kernel, at, mid // 2),
        grid_spec=pltpu.PrefetchScalarGridSpec(
            num_scalar_prefetch=1,
            grid=(rows // block,),
            in_specs=[
                pl.BlockSpec(memory_space=pltpu.SMEM),
                pl.BlockSpec((block, mid, phases), lambda i, c: (i, 0, 0)),
            ]
            + [WHOLE] * 5,
            out_specs=[out] * 2,
        ),
        out_shape=[jax.ShapeDtypeStruct((2, rows, size, phases), F32)] * 2,
        compiler_params=PARAMS,
        cost_estimate=LIGHT,
        name="local_terms",
    )(core, own_rows, occ, *c_split, b_both, row_b, row_c)


def first_kernel(n_slabs, n_deep, parity, fall, *refs):
    w_both, w_hi = refs[0], refs[1]
    slabs = refs[2 : 2 + n_slabs]
    deep = refs[2 + n_slabs : 2 + n_slabs + n_deep]
    mine, peer, stay_out, rise_out, swap_out = refs[2 + n_slabs + n_deep :]
    rows, span, lanes = stay_out.shape
    flat = [ref.reshape(ref.shape[0] * span, lanes) for ref in slabs]
    stay_flat = stay_out.reshape(rows * span, lanes)
    rise_flat = rise_out.reshape(rows * span, lanes)
    for b in range(0, span, 2):
        ats = [pl.ds(b, rows, stride=span), pl.ds(b + 1, rows, stride=span)]
        parts = []
        for ref in flat:
            picks = [pl.ds(b + n, ref.shape[0] // span, stride=span) for n in range(2)]
            parts.append(halves(jnp.concatenate([ref[pick, :] for pick in picks], axis=1)))
        g_hi = jnp.concatenate([p[0] for p in parts], axis=0)
        g_lo = jnp.concatenate([p[1] for p in parts], axis=0)
        both = dot(w_both[...], g_hi)
        out = both[: 2 * rows] + both[2 * rows :] + dot(w_hi[...], g_lo)
        for n, at in enumerate(ats):
            stay_flat[at, :] = out[:rows, n * lanes : (n + 1) * lanes]
            rise_flat[at, :] = out[rows:, n * lanes : (n + 1) * lanes]
    half = rows // 2
    once, twice = fall[0:1], fall[1:2]
    for which, near in enumerate((mine, peer)):
        part = slice(which * half, (which + 1) * half)
        far_down = deep[which][...] if n_deep == 2 else deep[0][part]
        stay_out[part] += near[0] + far_down * twice
        lift = rise_out[part] + near[1]
        rise_out[part] = lift

        @pl.when(parity[0] == 0)
        def _():
            swap_out[part] = lift + far_down * once

    @pl.when(parity[0] != 0)
    def _():
        at = 0
        for ref in slabs:
            if at < rows:
                swap_out[at : at + ref.shape[0]] = ref[...] * once
            at += ref.shape[0]


def first_terms(parity, fall, w_both, w_hi, slabs, deep, near, start):
    rows, size, phases = slabs[0].shape
    slab_specs = [pl.BlockSpec((v.shape[0], SPAN, LANES), lambda j, h: (0, j, h)) for v in [*slabs, *deep]]
    chunk = pl.BlockSpec((rows, SPAN, LANES), lambda j, h: (0, j, h))
    local_part = pl.BlockSpec((2, rows // 2, SPAN, LANES), lambda j, h: (0, 0, start // SPAN + j, h))
    return pl.pallas_call(
        functools.partial(first_kernel, len(slabs), len(deep)),
        grid=(size // SPAN, phases // LANES),
        in_specs=[pl.BlockSpec(memory_space=pltpu.SMEM), pl.BlockSpec((2, LANES), lambda j, h: (0, h)), WHOLE, WHOLE]
        + slab_specs
        + [local_part] * 2,
        out_specs=[chunk] * 3,
        out_shape=[jax.ShapeDtypeStruct((rows, size, phases), F32)] * 3,
        compiler_params=PARAMS,
        cost_estimate=LIGHT,
        name="first_terms",
    )(parity, fall, w_both, w_hi, *slabs, *deep, *near)


def turn_kernel(swap, lifted, out):
    out[...] = swap[...] + lifted[...]


def turn(swap, lifted):
    rows, size, phases = swap.shape
    block = max(8, rows // 2)
    chunk = pl.BlockSpec((block, SPAN, phases), lambda i, j: (i, j, 0))
    return pl.pallas_call(
        turn_kernel,
        grid=(rows // block, size // SPAN),
        in_specs=[chunk, chunk],
        out_specs=chunk,
        out_shape=jax.ShapeDtypeStruct(swap.shape, F32),
        compiler_params=PARAMS,
        cost_estimate=LIGHT,
        name="turn",
    )(swap, lifted)


def finish_kernel(n_alias, _, *refs):
    out, back = refs[4 + n_alias :]
    out[...] = refs[0][...] + refs[1][...]
    back[...] = refs[2][...] + refs[3][...]


def finish(core, out, back, shape, back_size, stay, risen, start, back_at):
    rows, size, phases = stay.shape
    half = rows // 2
    steps = shape[1] // 2 // SPAN
    args, specs = [core], []
    for which in range(2):
        for array in (stay, risen):
            args.append(array)
            specs.append(pl.BlockSpec((half, SPAN, LANES), lambda j, h, c, which=which: (which, j, h)))
    alias = {}
    for n, old in enumerate((out, back)):
        if old is not None:
            alias[len(args)] = n
            args.append(old)
            specs.append(pl.BlockSpec(memory_space=pl.ANY))
    return pl.pallas_call(
        functools.partial(finish_kernel, len(alias)),
        grid_spec=pltpu.PrefetchScalarGridSpec(
            num_scalar_prefetch=1,
            grid=(size // SPAN, phases // LANES),
            in_specs=specs,
            out_specs=[
                pl.BlockSpec((half, SPAN, LANES), lambda j, h, c: (0, c[0] * steps + start // SPAN + j, h)),
                pl.BlockSpec((half, SPAN, LANES), lambda j, h, c: (0, back_at // SPAN + j, h)),
            ],
        ),
        out_shape=[jax.ShapeDtypeStruct(shape, F32), jax.ShapeDtypeStruct((half, back_size, phases), F32)],
        input_output_aliases=alias,
        compiler_params=PARAMS,
        cost_estimate=LIGHT,
        name="finish",
    )(*args)


def put_kernel(core, piece, _, out):
    out[...] = piece[...]


def put(core, out, piece, start):
    rows, size, phases = piece.shape
    steps = out.shape[1] // 2 // SPAN
    return pl.pallas_call(
        put_kernel,
        grid_spec=pltpu.PrefetchScalarGridSpec(
            num_scalar_prefetch=1,
            grid=(size // SPAN,),
            in_specs=[
                pl.BlockSpec((rows, SPAN, phases), lambda j, c: (0, j, 0)),
                pl.BlockSpec(memory_space=pl.ANY),
            ],
            out_specs=pl.BlockSpec((rows, SPAN, phases), lambda j, c: (0, c[1] * steps + start // SPAN + j, 0)),
        ),
        out_shape=jax.ShapeDtypeStruct(out.shape, F32),
        input_output_aliases={2: 0},
        compiler_params=PARAMS,
        cost_estimate=LIGHT,
        name="put",
    )(core, piece, out)


def local(occupancy, rates, increments, draw, crusher_rate, bounds):
    n_cls, n_lvl = lax.axis_size("cls"), lax.axis_size("lvl")
    occ = occupancy[0]
    rows, mid, phases = occ.shape
    half = mid // 2
    level = lax.axis_index("lvl")
    place = lax.axis_index("cls")
    k = place % 2
    core = jnp.stack([k, 1 - k])
    even = level % 2 == 0
    bottom, top = bounds[0], bounds[1]

    def along_cls(v, by):
        return lax.ppermute(v, "cls", [(i, (i + by) % n_cls) for i in range(n_cls)])

    def other_core(v):
        return lax.ppermute(v, "cls", [(i, i ^ 1) for i in range(n_cls)])

    def two_down(v):
        return lax.ppermute(v, "lvl", [(i, i - 2) for i in range(2, n_lvl)])

    def two_up(v):
        return lax.ppermute(v, "lvl", [(i, i + 2) for i in range(1, n_lvl - 2, 2)])

    def pair_swap(v):
        return lax.ppermute(v, "lvl", [(i, i ^ 1) for i in range(n_lvl)])

    def cut(array, which, at, size):
        return lax.dynamic_slice_in_dim(array, core[which] * half + at, size, axis=1)

    chunks, groups = plan(rows, half)
    n = len(chunks)
    size = chunks[0][1]
    shifts = [2 * s for s in range(1, n_cls // 2)]
    sent = [None] * n
    tokens = []
    for lo, hi in spans(*sorted({0, n // 4, n})):
        at = chunks[lo][0]
        give = cut(occ, 1, at, (hi - lo) * size)
        if tokens:
            give, _ = gate(give, tokens[-1])
        got = other_core(give)
        tokens.append(got)
        for s in range(lo, hi):
            start = chunks[s][0]
            part = lax.slice_in_dim(got, start - at, start - at + size, axis=1)
            sent[s] = jnp.concatenate([cut(occ, 0, start, size), part], axis=0)

    far, deep = [None] * n, [None] * n

    def start_early(s):
        for by in shifts:
            straight = along_cls(cut(occ, 0, s * size, size), by)
            crossed = [(i, ((i + by) % n_cls) ^ 1) for i in range(n_cls)]
            cross = lax.ppermute(cut(occ, 1, s * size, size), "cls", crossed)
            far[s] = (far[s] or []) + [straight, cross]
        both = [(i * n_lvl + m, (i ^ 1) * n_lvl + m - 2) for i in range(n_cls) for m in range(2, n_lvl)]
        deep[s] = [two_down(cut(occ, 0, s * size, size)), lax.ppermute(cut(occ, 1, s * size, size), ("cls", "lvl"), both)]

    def start_far(s, *after):
        operand = gate(sent[s], *after)[0] if after else sent[s]
        far[s] = [along_cls(operand, by) for by in shifts]

    def start_deep(s, *after):
        operand = gate(sent[s], *after)[0] if after else sent[s]
        deep[s] = [two_down(operand)]

    start_early(0)

    row_total = jnp.sum(rates, axis=2)
    uniform_rate = jnp.sum(jnp.max(row_total, axis=1)) + jnp.max(crusher_rate)
    out_rows = row_total * flag((increments == 0) | (level + increments <= top))
    rise_ok = flag(level + 1 <= top)
    drop_here = crusher_rate * flag(level - draw >= bottom)
    drop_deep = crusher_rate * flag(level + 2 - draw >= bottom)
    scale = 1.0 / uniform_rate
    once = jnp.where(even, drop_deep, drop_here) * flag(draw == 1) * scale
    twice = drop_deep * flag(draw == 2) * scale
    fall_vec = jnp.stack([once, twice])
    parity = (level % 2)[None]

    stay_rows = rates * (flag(increments == 0) * scale)[:, :, None]
    rise_rows = rates * (flag(increments == 1) * (rise_ok * scale))[:, :, None]

    c_split = halves_outside(jnp.concatenate([stay_rows[2], rise_rows[2]], axis=1))
    lost = out_rows * scale
    own_rows = lax.dynamic_slice_in_dim(lost[0], place * rows, rows)
    row_c = (1.0 - lost[2] - drop_here * scale)[None, :]
    parts = []

    def start_part(lo, hi, begin):
        at, span = chunks[lo][0], (hi - lo) * size
        cat_b = jnp.concatenate([cut(r, w, at, span) for r in (stay_rows[1], rise_rows[1]) for w in range(2)], axis=1)
        row_b = jnp.concatenate([lax.dynamic_slice_in_dim(lost[1], core[w] * half + at, span) for w in range(2)])
        mine, give = local_terms(
            core,
            gate(occ, begin)[0],
            own_rows,
            c_split,
            jnp.concatenate(halves_outside(cat_b.T), axis=0),
            row_b[:, None],
            row_c,
            at,
            span,
        )
        return lo, hi, at, mine, give

    def send_part(part, *after):
        lo, hi, at, mine, give = part
        parts.append((lo, hi, at, (mine, other_core(gate(give, *after)[0]))))

    first_rows = 3 * n // 16 if n > 8 else n
    send_part(start_part(0, first_rows, tokens[0]), *far[0], *deep[0])
    waiting = {}
    later = {0: (first_rows, n // 2), n // 2 - 4: (n // 2, n)} if n > 8 else {}

    origin = [place, place ^ 1]
    for by in shifts:
        origin += [(place - by) % n_cls, ((place - by) % n_cls) ^ 1]
    mine = jnp.concatenate(
        [
            lax.dynamic_slice_in_dim(r, p * rows, rows, axis=1)
            for r in (stay_rows[0], rise_rows[0])
            for p in (place, place ^ 1)
        ],
        axis=1,
    ).T
    mine = jnp.concatenate([lax.dynamic_slice_in_dim(mine, o * rows, rows, axis=1) for o in origin], axis=1)
    a_hi, a_lo = halves_outside(mine)
    a_both = jnp.concatenate([a_hi, a_lo], axis=0)

    out = None
    stay, rise, swap, lifted, risen = ([None] * n for _ in range(5))
    back = [None] * len(groups)
    group_of = {s: g for g, (lo, hi) in enumerate(groups) for s in range(lo, hi)}

    for s in range(n + 4):
        if s < n:
            if s >= 3:
                far[s][0], risen[s - 3] = gate(far[s][0], risen[s - 3])
            if s >= 4:
                far[s][0], out = gate(far[s][0], out)
            if s + 1 < n:
                start_far(s + 1, far[s][0])
            if s + 1 < n:
                start_deep(s + 1, far[s][0], *deep[s])
            lo, hi, at, near = next(p for p in parts if p[0] <= s < p[1])
            stay[s], rise[s], swap[s] = first_terms(
                parity, fall_vec, a_both, a_hi, [sent[s]] + far[s], deep[s], near, chunks[s][0] - at
            )
            lift_me = rise[s]
            if s >= 1:
                lift_me, lifted[s - 1] = gate(lift_me, lifted[s - 1])
            lifted[s] = two_up(lift_me)
        if 1 <= s <= n:
            p = s - 1
            swap_me = turn(swap[p], lifted[p])
            if p in later:
                waiting[p + 2] = start_part(*later[p], swap_me)
            if p >= 1:
                swap_me, risen[p - 1] = gate(swap_me, risen[p - 1])
            risen[p] = pair_swap(swap_me)
            if s in waiting:
                send_part(waiting[s], *far[s], *deep[s], lifted[p], risen[p - 1])
        if 0 <= s - 2 < n:
            p = s - 2
            g = group_of[p]
            lo, hi = groups[g]
            out, back[g] = finish(
                core, out, back[g], occ.shape, (hi - lo) * size, stay[p], risen[p], chunks[p][0], (p - lo) * size
            )
            if p == hi - 1:
                back[g] = other_core(back[g])
        if 0 <= s - 3 < n:
            p = s - 3
            lo, hi = groups[group_of[p]]
            if p == hi - 1:
                out = put(core, out, back[group_of[p]], chunks[lo][0])
    return out[None]


def solution(mesh):
    in_specs = (P("lvl", "cls", None, None), P(), P(), P(), P(), P())
    out_specs = P("lvl", "cls", None, None)
    return jax.shard_map(local, mesh=mesh, in_specs=in_specs, out_specs=out_specs, check_vma=False)
```

```python
import functools

import jax
import jax.numpy as jnp
from jax import lax
from jax.experimental import pallas as pl
from jax.experimental.pallas import tpu as pltpu
from jax.sharding import PartitionSpec as P

F32 = jnp.float32
BF16 = jnp.bfloat16
VMEM_LIMIT = 56 * 2**20
SPAN, LANES = 8, 128
LIGHT = pl.CostEstimate(flops=1000, transcendentals=0, bytes_accessed=1000)
PARAMS = pltpu.CompilerParams(vmem_limit_bytes=VMEM_LIMIT)
WHOLE = pl.BlockSpec(memory_space=pltpu.VMEM)


def gate(*values):
    return lax.optimization_barrier(values)


def flag(cond):
    return jnp.where(cond, 1.0, 0.0).astype(F32)


def halves(x):
    high = x.astype(BF16)
    low = (x - high.astype(F32)).astype(BF16)
    return high, low


def halves_outside(x):
    high = lax.reduce_precision(x, 8, 7)
    return high.astype(BF16), (x - high).astype(BF16)


def dot(a, b):
    return jnp.dot(a, b, preferred_element_type=F32)


def plan(rows, length):
    n = max(4, rows // 8)
    size = length // n
    chunks = [(s * size, size) for s in range(n)]
    return chunks, [(0, n - 2), (n - 2, n - 1), (n - 1, n)]


def spans(*bounds):
    return list(zip(bounds[:-1], bounds[1:]))


def local_kernel(at, half, core, own_rows, occ, c_hi, c_lo, b_both, row_b, row_c, *outs):
    block, phases = occ.shape[0], occ.shape[2]
    size = outs[0].shape[2]
    first = pl.program_id(0) * block
    rows = [pl.ds(pl.multiple_of(core[n] * half + at, SPAN), size) for n in range(2)]
    y = jnp.concatenate([occ[i, r] for i in range(block) for r in rows], axis=0)
    y_hi, y_lo = halves(y)
    n_y = y.shape[0]
    by_c = dot(jnp.concatenate([y_hi, y_lo], axis=0), c_hi[...])
    by_c = by_c[:n_y] + by_c[n_y:] + dot(y_hi, c_lo[...])
    for i in range(block):
        x_hi, x_lo = halves(occ[i])
        by_b = dot(b_both[...], x_hi)
        by_b = by_b[: 4 * size] + by_b[4 * size :] + dot(b_both[: 4 * size], x_lo)
        here = slice(2 * size * i, 2 * size * (i + 1))
        left = row_c[...] - own_rows[first + i] - row_b[...]
        base = by_c[here, :phases] + by_b[: 2 * size] + y[here] * left
        rise = by_c[here, phases:] + by_b[2 * size :]
        mine, peer = outs
        for n, value in enumerate((base, rise)):
            mine[n, i] = value[:size]
            peer[n, i] = value[size:]


def local_terms(core, occ, own_rows, c_split, b_both, row_b, row_c, at, size):
    rows, mid, phases = occ.shape
    block = 8
    out = pl.BlockSpec((2, block, size, phases), lambda i, c: (0, i, 0, 0))
    return pl.pallas_call(
        functools.partial(local_kernel, at, mid // 2),
        grid_spec=pltpu.PrefetchScalarGridSpec(
            num_scalar_prefetch=1,
            grid=(rows // block,),
            in_specs=[
                pl.BlockSpec(memory_space=pltpu.SMEM),
                pl.BlockSpec((block, mid, phases), lambda i, c: (i, 0, 0)),
            ]
            + [WHOLE] * 5,
            out_specs=[out] * 2,
        ),
        out_shape=[jax.ShapeDtypeStruct((2, rows, size, phases), F32)] * 2,
        compiler_params=PARAMS,
        cost_estimate=LIGHT,
        name="local_terms",
    )(core, own_rows, occ, *c_split, b_both, row_b, row_c)


def first_kernel(n_slabs, n_deep, parity, fall, *refs):
    w_both, w_hi = refs[0], refs[1]
    slabs = refs[2 : 2 + n_slabs]
    deep = refs[2 + n_slabs : 2 + n_slabs + n_deep]
    mine, peer, stay_out, rise_out, swap_out = refs[2 + n_slabs + n_deep :]
    rows, span, lanes = stay_out.shape
    flat = [ref.reshape(ref.shape[0] * span, lanes) for ref in slabs]
    stay_flat = stay_out.reshape(rows * span, lanes)
    rise_flat = rise_out.reshape(rows * span, lanes)
    for b in range(0, span, 2):
        ats = [pl.ds(b, rows, stride=span), pl.ds(b + 1, rows, stride=span)]
        parts = []
        for ref in flat:
            picks = [pl.ds(b + n, ref.shape[0] // span, stride=span) for n in range(2)]
            parts.append(halves(jnp.concatenate([ref[pick, :] for pick in picks], axis=1)))
        g_hi = jnp.concatenate([p[0] for p in parts], axis=0)
        g_lo = jnp.concatenate([p[1] for p in parts], axis=0)
        both = dot(w_both[...], g_hi)
        out = both[: 2 * rows] + both[2 * rows :] + dot(w_hi[...], g_lo)
        for n, at in enumerate(ats):
            stay_flat[at, :] = out[:rows, n * lanes : (n + 1) * lanes]
            rise_flat[at, :] = out[rows:, n * lanes : (n + 1) * lanes]
    half = rows // 2
    once, twice = fall[0:1], fall[1:2]
    for which, near in enumerate((mine, peer)):
        part = slice(which * half, (which + 1) * half)
        far_down = deep[which][...] if n_deep == 2 else deep[0][part]
        stay_out[part] += near[0] + far_down * twice
        lift = rise_out[part] + near[1]
        rise_out[part] = lift

        @pl.when(parity[0] == 0)
        def _():
            swap_out[part] = lift + far_down * once

    @pl.when(parity[0] != 0)
    def _():
        at = 0
        for ref in slabs:
            if at < rows:
                swap_out[at : at + ref.shape[0]] = ref[...] * once
            at += ref.shape[0]


def first_terms(parity, fall, w_both, w_hi, slabs, deep, near, start):
    rows, size, phases = slabs[0].shape
    slab_specs = [pl.BlockSpec((v.shape[0], SPAN, LANES), lambda j, h: (0, j, h)) for v in [*slabs, *deep]]
    chunk = pl.BlockSpec((rows, SPAN, LANES), lambda j, h: (0, j, h))
    local_part = pl.BlockSpec((2, rows // 2, SPAN, LANES), lambda j, h: (0, 0, start // SPAN + j, h))
    return pl.pallas_call(
        functools.partial(first_kernel, len(slabs), len(deep)),
        grid=(size // SPAN, phases // LANES),
        in_specs=[pl.BlockSpec(memory_space=pltpu.SMEM), pl.BlockSpec((2, LANES), lambda j, h: (0, h)), WHOLE, WHOLE]
        + slab_specs
        + [local_part] * 2,
        out_specs=[chunk] * 3,
        out_shape=[jax.ShapeDtypeStruct((rows, size, phases), F32)] * 3,
        compiler_params=PARAMS,
        cost_estimate=LIGHT,
        name="first_terms",
    )(parity, fall, w_both, w_hi, *slabs, *deep, *near)


def turn_kernel(swap, lifted, out):
    out[...] = swap[...] + lifted[...]


def turn(swap, lifted):
    rows, size, phases = swap.shape
    block = max(8, rows // 2)
    chunk = pl.BlockSpec((block, SPAN, phases), lambda i, j: (i, j, 0))
    return pl.pallas_call(
        turn_kernel,
        grid=(rows // block, size // SPAN),
        in_specs=[chunk, chunk],
        out_specs=chunk,
        out_shape=jax.ShapeDtypeStruct(swap.shape, F32),
        compiler_params=PARAMS,
        cost_estimate=LIGHT,
        name="turn",
    )(swap, lifted)


def finish_kernel(n_alias, _, *refs):
    out, back = refs[4 + n_alias :]
    out[...] = refs[0][...] + refs[1][...]
    back[...] = refs[2][...] + refs[3][...]


def finish(core, out, back, shape, back_size, stay, risen, start, back_at):
    rows, size, phases = stay.shape
    half = rows // 2
    steps = shape[1] // 2 // SPAN
    args, specs = [core], []
    for which in range(2):
        for array in (stay, risen):
            args.append(array)
            specs.append(pl.BlockSpec((half, SPAN, LANES), lambda j, h, c, which=which: (which, j, h)))
    alias = {}
    for n, old in enumerate((out, back)):
        if old is not None:
            alias[len(args)] = n
            args.append(old)
            specs.append(pl.BlockSpec(memory_space=pl.ANY))
    return pl.pallas_call(
        functools.partial(finish_kernel, len(alias)),
        grid_spec=pltpu.PrefetchScalarGridSpec(
            num_scalar_prefetch=1,
            grid=(size // SPAN, phases // LANES),
            in_specs=specs,
            out_specs=[
                pl.BlockSpec((half, SPAN, LANES), lambda j, h, c: (0, c[0] * steps + start // SPAN + j, h)),
                pl.BlockSpec((half, SPAN, LANES), lambda j, h, c: (0, back_at // SPAN + j, h)),
            ],
        ),
        out_shape=[jax.ShapeDtypeStruct(shape, F32), jax.ShapeDtypeStruct((half, back_size, phases), F32)],
        input_output_aliases=alias,
        compiler_params=PARAMS,
        cost_estimate=LIGHT,
        name="finish",
    )(*args)


def put_kernel(core, piece, _, out):
    out[...] = piece[...]


def put(core, out, piece, start):
    rows, size, phases = piece.shape
    steps = out.shape[1] // 2 // SPAN
    return pl.pallas_call(
        put_kernel,
        grid_spec=pltpu.PrefetchScalarGridSpec(
            num_scalar_prefetch=1,
            grid=(size // SPAN,),
            in_specs=[
                pl.BlockSpec((rows, SPAN, phases), lambda j, c: (0, j, 0)),
                pl.BlockSpec(memory_space=pl.ANY),
            ],
            out_specs=pl.BlockSpec((rows, SPAN, phases), lambda j, c: (0, c[1] * steps + start // SPAN + j, 0)),
        ),
        out_shape=jax.ShapeDtypeStruct(out.shape, F32),
        input_output_aliases={2: 0},
        compiler_params=PARAMS,
        cost_estimate=LIGHT,
        name="put",
    )(core, piece, out)


def local(occupancy, rates, increments, draw, crusher_rate, bounds):
    n_cls, n_lvl = lax.axis_size("cls"), lax.axis_size("lvl")
    occ = occupancy[0]
    rows, mid, phases = occ.shape
    half = mid // 2
    level = lax.axis_index("lvl")
    place = lax.axis_index("cls")
    k = place % 2
    core = jnp.stack([k, 1 - k])
    even = level % 2 == 0
    bottom, top = bounds[0], bounds[1]

    def along_cls(v, by):
        return lax.ppermute(v, "cls", [(i, (i + by) % n_cls) for i in range(n_cls)])

    def other_core(v):
        return lax.ppermute(v, "cls", [(i, i ^ 1) for i in range(n_cls)])

    def two_down(v):
        return lax.ppermute(v, "lvl", [(i, i - 2) for i in range(2, n_lvl)])

    def two_up(v):
        return lax.ppermute(v, "lvl", [(i, i + 2) for i in range(1, n_lvl - 2, 2)])

    def pair_swap(v):
        return lax.ppermute(v, "lvl", [(i, i ^ 1) for i in range(n_lvl)])

    def cut(array, which, at, size):
        return lax.dynamic_slice_in_dim(array, core[which] * half + at, size, axis=1)

    chunks, groups = plan(rows, half)
    n = len(chunks)
    size = chunks[0][1]
    shifts = [2 * s for s in range(1, n_cls // 2)]
    sent = [None] * n
    tokens = []
    for lo, hi in spans(*sorted({0, n // 4, n})):
        at = chunks[lo][0]
        give = cut(occ, 1, at, (hi - lo) * size)
        if tokens:
            give, _ = gate(give, tokens[-1])
        got = other_core(give)
        tokens.append(got)
        for s in range(lo, hi):
            start = chunks[s][0]
            part = lax.slice_in_dim(got, start - at, start - at + size, axis=1)
            sent[s] = jnp.concatenate([cut(occ, 0, start, size), part], axis=0)

    far, deep = [None] * n, [None] * n

    def start_early(s):
        for by in shifts:
            straight = along_cls(cut(occ, 0, s * size, size), by)
            crossed = [(i, ((i + by) % n_cls) ^ 1) for i in range(n_cls)]
            cross = lax.ppermute(cut(occ, 1, s * size, size), "cls", crossed)
            far[s] = (far[s] or []) + [straight, cross]
        both = [(i * n_lvl + m, (i ^ 1) * n_lvl + m - 2) for i in range(n_cls) for m in range(2, n_lvl)]
        deep[s] = [two_down(cut(occ, 0, s * size, size)), lax.ppermute(cut(occ, 1, s * size, size), ("cls", "lvl"), both)]

    def start_far(s, *after):
        operand = gate(sent[s], *after)[0] if after else sent[s]
        far[s] = [along_cls(operand, by) for by in shifts]

    def start_deep(s, *after):
        operand = gate(sent[s], *after)[0] if after else sent[s]
        deep[s] = [two_down(operand)]

    start_early(0)

    row_total = jnp.sum(rates, axis=2)
    uniform_rate = jnp.sum(jnp.max(row_total, axis=1)) + jnp.max(crusher_rate)
    out_rows = row_total * flag((increments == 0) | (level + increments <= top))
    rise_ok = flag(level + 1 <= top)
    drop_here = crusher_rate * flag(level - draw >= bottom)
    drop_deep = crusher_rate * flag(level + 2 - draw >= bottom)
    scale = 1.0 / uniform_rate
    once = jnp.where(even, drop_deep, drop_here) * flag(draw == 1) * scale
    twice = drop_deep * flag(draw == 2) * scale
    fall_vec = jnp.stack([once, twice])
    parity = (level % 2)[None]

    stay_rows = rates * (flag(increments == 0) * scale)[:, :, None]
    rise_rows = rates * (flag(increments == 1) * (rise_ok * scale))[:, :, None]

    c_split = halves_outside(jnp.concatenate([stay_rows[2], rise_rows[2]], axis=1))
    lost = out_rows * scale
    own_rows = lax.dynamic_slice_in_dim(lost[0], place * rows, rows)
    row_c = (1.0 - lost[2] - drop_here * scale)[None, :]
    parts = []

    def start_part(lo, hi, begin):
        at, span = chunks[lo][0], (hi - lo) * size
        cat_b = jnp.concatenate([cut(r, w, at, span) for r in (stay_rows[1], rise_rows[1]) for w in range(2)], axis=1)
        row_b = jnp.concatenate([lax.dynamic_slice_in_dim(lost[1], core[w] * half + at, span) for w in range(2)])
        mine, give = local_terms(
            core,
            gate(occ, begin)[0],
            own_rows,
            c_split,
            jnp.concatenate(halves_outside(cat_b.T), axis=0),
            row_b[:, None],
            row_c,
            at,
            span,
        )
        return lo, hi, at, mine, give

    def send_part(part, *after):
        lo, hi, at, mine, give = part
        parts.append((lo, hi, at, (mine, other_core(gate(give, *after)[0]))))

    first_rows = 3 if n > 4 else n
    send_part(start_part(0, first_rows, tokens[0]), *far[0], *deep[0])
    waiting = {}
    later = {0: (first_rows, n)} if n > 4 else {}

    origin = [place, place ^ 1]
    for by in shifts:
        origin += [(place - by) % n_cls, ((place - by) % n_cls) ^ 1]
    mine = jnp.concatenate(
        [
            lax.dynamic_slice_in_dim(r, p * rows, rows, axis=1)
            for r in (stay_rows[0], rise_rows[0])
            for p in (place, place ^ 1)
        ],
        axis=1,
    ).T
    mine = jnp.concatenate([lax.dynamic_slice_in_dim(mine, o * rows, rows, axis=1) for o in origin], axis=1)
    a_hi, a_lo = halves_outside(mine)
    a_both = jnp.concatenate([a_hi, a_lo], axis=0)

    out = None
    stay, rise, swap, lifted, risen = ([None] * n for _ in range(5))
    back = [None] * len(groups)
    group_of = {s: g for g, (lo, hi) in enumerate(groups) for s in range(lo, hi)}

    for s in range(n + 4):
        if s < n:
            if s >= 3:
                far[s][0], risen[s - 3] = gate(far[s][0], risen[s - 3])
            if s >= 4:
                far[s][0], out = gate(far[s][0], out)
            if s + 1 < n:
                start_far(s + 1, far[s][0])
            if s + 1 < n:
                start_deep(s + 1, far[s][0], *deep[s])
            lo, hi, at, near = next(p for p in parts if p[0] <= s < p[1])
            stay[s], rise[s], swap[s] = first_terms(
                parity, fall_vec, a_both, a_hi, [sent[s]] + far[s], deep[s], near, chunks[s][0] - at
            )
            lift_me = rise[s]
            if s >= 1:
                lift_me, lifted[s - 1] = gate(lift_me, lifted[s - 1])
            lifted[s] = two_up(lift_me)
        if 1 <= s <= n:
            p = s - 1
            swap_me = turn(swap[p], lifted[p])
            if p in later:
                waiting[p + 2] = start_part(*later[p], swap_me)
            if p >= 1:
                swap_me, risen[p - 1] = gate(swap_me, risen[p - 1])
            risen[p] = pair_swap(swap_me)
            if s in waiting:
                send_part(waiting[s], *far[s], *deep[s], lifted[p], risen[p - 1])
        if 0 <= s - 2 < n:
            p = s - 2
            g = group_of[p]
            lo, hi = groups[g]
            out, back[g] = finish(
                core, out, back[g], occ.shape, (hi - lo) * size, stay[p], risen[p], chunks[p][0], (p - lo) * size
            )
            if p == hi - 1:
                back[g] = other_core(back[g])
        if 0 <= s - 3 < n:
            p = s - 3
            lo, hi = groups[group_of[p]]
            if p == hi - 1:
                out = put(core, out, back[group_of[p]], chunks[lo][0])
    return out[None]


def solution(mesh):
    in_specs = (P("lvl", "cls", None, None), P(), P(), P(), P(), P())
    out_specs = P("lvl", "cls", None, None)
    return jax.shard_map(local, mesh=mesh, in_specs=in_specs, out_specs=out_specs, check_vma=False)
```

```python
import functools

import jax
import jax.numpy as jnp
from jax import lax
from jax.experimental import pallas as pl
from jax.experimental.pallas import tpu as pltpu
from jax.sharding import PartitionSpec as P

F32 = jnp.float32
BF16 = jnp.bfloat16
VMEM_LIMIT = 56 * 2**20
SPAN, LANES = 8, 128
FIRST_ROWS = 1
LIGHT = pl.CostEstimate(flops=1000, transcendentals=0, bytes_accessed=1000)
PARAMS = pltpu.CompilerParams(vmem_limit_bytes=VMEM_LIMIT)
WHOLE = pl.BlockSpec(memory_space=pltpu.VMEM)


def gate(*values):
    return lax.optimization_barrier(values)


def flag(cond):
    return jnp.where(cond, 1.0, 0.0).astype(F32)


def halves(x):
    high = x.astype(BF16)
    low = (x - high.astype(F32)).astype(BF16)
    return high, low


def halves_outside(x):
    high = lax.reduce_precision(x, 8, 7)
    return high.astype(BF16), (x - high).astype(BF16)


def dot(a, b):
    return jnp.dot(a, b, preferred_element_type=F32)


def plan(rows, length):
    n = max(4, rows // 8)
    size = length // n
    chunks = [(s * size, size) for s in range(n)]
    return chunks, [(0, n - 2), (n - 2, n - 1), (n - 1, n)]


def spans(*bounds):
    return list(zip(bounds[:-1], bounds[1:]))


def prepare_kernel(rows, where, bounds, rates, inc_rows, inc_cols, draw, crusher, a_out, c_hi, c_lo, b_hi, b_lo, lost_a, lost_b,
                   left_c, fall, flip):
    level = where[2]
    top, bottom = bounds[1], bounds[0]
    phases = rates.shape[1]
    totals = [jnp.sum(rates[c], axis=1, keepdims=True) for c in range(3)]
    uniform = jnp.max(crusher[...], axis=1, keepdims=True)
    for total in totals:
        uniform = uniform + jnp.max(total, axis=0, keepdims=True)
    scale = 1.0 / uniform
    rise_ok = jnp.where(level + 1 <= top, 1.0, 0.0)

    def opened(inc):
        return jnp.where((inc == 0) | (level + inc <= top), 1.0, 0.0)

    def masks(inc):
        return [jnp.where(inc == 0, 1.0, 0.0) * scale, jnp.where(inc == 1, 1.0, 0.0) * (rise_ok * scale)]

    lost_a[...] = totals[0] * opened(inc_cols[0]) * scale
    lost_b[...] = totals[1] * opened(inc_cols[1]) * scale
    total_c = jnp.sum(jnp.transpose(rates[2]), axis=0, keepdims=True)
    here = crusher[...] * jnp.where(level - draw[...] >= bottom, 1.0, 0.0)
    deep = crusher[...] * jnp.where(level + 2 - draw[...] >= bottom, 1.0, 0.0)
    left_c[...] = 1.0 - total_c * opened(inc_rows[2:3]) * scale - here * scale
    fall[0:1] = jnp.where(level % 2 == 0, deep, here) * jnp.where(draw[...] == 1, 1.0, 0.0) * scale
    fall[1:2] = deep * jnp.where(draw[...] == 2, 1.0, 0.0) * scale
    for n, mask in enumerate(masks(inc_cols[2])):
        high, low = halves(rates[2] * mask)
        c_hi[:, n * phases : (n + 1) * phases] = high
        c_lo[:, n * phases : (n + 1) * phases] = low
    for n, mask in enumerate(masks(inc_cols[1])):
        high, low = halves(jnp.transpose(rates[1] * mask))
        b_hi[n] = high
        b_lo[n] = low
    spots = [pl.ds(pl.multiple_of(where[3 + n] * rows, 8), rows) for n in range(phases // rows)]
    ordered = jnp.concatenate([rates[0, spot] for spot in spots], axis=0)
    inc = jnp.concatenate([inc_cols[0, spot] for spot in spots], axis=0)
    for n, mask in enumerate(masks(inc)):
        flip[...] = jnp.transpose(ordered * mask)
        for which in range(2):
            at = (2 * n + which) * rows
            high, low = halves(flip[spots[which]])
            a_out[at : at + rows] = high
            a_out[4 * rows + at : 5 * rows + at] = low


def prepare(where, bounds, rates, increments, draw, crusher_rate, rows):
    phases = rates.shape[1]
    smem = pl.BlockSpec(memory_space=pltpu.SMEM)
    shapes = [
        ((8 * rows, phases), BF16),
        ((phases, 2 * phases), BF16),
        ((phases, 2 * phases), BF16),
        ((2, phases, phases), BF16),
        ((2, phases, phases), BF16),
        ((phases, 1), F32),
        ((phases, 1), F32),
        ((1, phases), F32),
        ((2, phases), F32),
    ]
    return pl.pallas_call(
        functools.partial(prepare_kernel, rows),
        in_specs=[smem, smem] + [WHOLE] * 5,
        out_specs=[WHOLE] * len(shapes),
        out_shape=[jax.ShapeDtypeStruct(*v) for v in shapes],
        scratch_shapes=[pltpu.VMEM((phases, phases), F32)],
        compiler_params=PARAMS,
        cost_estimate=LIGHT,
        name="prepare",
    )(where, bounds, rates, increments, increments[:, :, None], draw[None], crusher_rate[None])


def local_kernel(at, half, where, lost_a, occ, c_hi, c_lo, b_hi, b_lo, lost_b, left_c, mine, peer, b_both, left_b):
    block, phases = occ.shape[0], occ.shape[2]
    size = mine.shape[2]
    rows = [pl.ds(pl.multiple_of(where[n] * half + at, 16), size) for n in range(2)]

    @pl.when(pl.program_id(0) == 0)
    def _():
        for n in range(2):
            left_b[n * size : (n + 1) * size] = lost_b[rows[n]]
            for m in range(2):
                spot = (2 * m + n) * size
                b_both[spot : spot + size] = b_hi[m, rows[n]]
                b_both[4 * size + spot : 5 * size + spot] = b_lo[m, rows[n]]

    first = where[3] * (pl.num_programs(0) * block) + pl.program_id(0) * block
    y = jnp.concatenate([occ[i, r] for i in range(block) for r in rows], axis=0)
    y_hi, y_lo = halves(y)
    n_y = y.shape[0]
    by_c = dot(jnp.concatenate([y_hi, y_lo], axis=0), c_hi[...])
    by_c = by_c[:n_y] + by_c[n_y:] + dot(y_hi, c_lo[...])
    for i in range(block):
        x_hi, x_lo = halves(occ[i])
        by_b = dot(b_both[...], x_hi)
        by_b = by_b[: 4 * size] + by_b[4 * size :] + dot(b_both[: 4 * size], x_lo)
        here = slice(2 * size * i, 2 * size * (i + 1))
        left = left_c[...] - lost_a[pl.ds(first + i, 1)] - left_b[...]
        base = by_c[here, :phases] + by_b[: 2 * size] + y[here] * left
        rise = by_c[here, phases:] + by_b[2 * size :]
        for n, value in enumerate((base, rise)):
            mine[n, i] = value[:size]
            peer[n, i] = value[size:]


def local_terms(where, occ, lost_a, factors, at, size):
    rows, mid, phases = occ.shape
    block = 8
    out = pl.BlockSpec((2, block, size, phases), lambda i, c: (0, i, 0, 0))
    return pl.pallas_call(
        functools.partial(local_kernel, at, mid // 2),
        grid_spec=pltpu.PrefetchScalarGridSpec(
            num_scalar_prefetch=1,
            grid=(rows // block,),
            in_specs=[WHOLE, pl.BlockSpec((block, mid, phases), lambda i, c: (i, 0, 0))] + [WHOLE] * len(factors),
            out_specs=[out] * 2,
            scratch_shapes=[pltpu.VMEM((8 * size, mid), BF16), pltpu.VMEM((2 * size, 1), F32)],
        ),
        out_shape=[jax.ShapeDtypeStruct((2, rows, size, phases), F32)] * 2,
        compiler_params=PARAMS,
        cost_estimate=LIGHT,
        name="local_terms",
    )(where, lost_a, occ, *factors)


def first_kernel(n_slabs, n_deep, where, fall, *refs):
    w_both = refs[0]
    slabs = refs[1 : 1 + n_slabs]
    deep = refs[1 + n_slabs : 1 + n_slabs + n_deep]
    mine, peer, stay_out, rise_out, swap_out = refs[1 + n_slabs + n_deep :]
    rows, span, lanes = stay_out.shape
    flat = [ref.reshape(ref.shape[0] * span, lanes) for ref in slabs]
    stay_flat = stay_out.reshape(rows * span, lanes)
    rise_flat = rise_out.reshape(rows * span, lanes)
    for b in range(0, span, 2):
        ats = [pl.ds(b, rows, stride=span), pl.ds(b + 1, rows, stride=span)]
        parts = []
        for ref in flat:
            picks = [pl.ds(b + n, ref.shape[0] // span, stride=span) for n in range(2)]
            parts.append(halves(jnp.concatenate([ref[pick, :] for pick in picks], axis=1)))
        g_hi = jnp.concatenate([p[0] for p in parts], axis=0)
        g_lo = jnp.concatenate([p[1] for p in parts], axis=0)
        both = dot(w_both[...], g_hi)
        out = both[: 2 * rows] + both[2 * rows :] + dot(w_both[: 2 * rows], g_lo)
        for n, at in enumerate(ats):
            stay_flat[at, :] = out[:rows, n * lanes : (n + 1) * lanes]
            rise_flat[at, :] = out[rows:, n * lanes : (n + 1) * lanes]
    half = rows // 2
    once, twice = fall[0:1], fall[1:2]
    for which, near in enumerate((mine, peer)):
        part = slice(which * half, (which + 1) * half)
        far_down = deep[which][...] if n_deep == 2 else deep[0][part]
        stay_out[part] += near[0] + far_down * twice
        lift = rise_out[part] + near[1]
        rise_out[part] = lift

        @pl.when(where[2] % 2 == 0)
        def _():
            swap_out[part] = lift + far_down * once

    @pl.when(where[2] % 2 != 0)
    def _():
        at = 0
        for ref in slabs:
            if at < rows:
                swap_out[at : at + ref.shape[0]] = ref[...] * once
            at += ref.shape[0]


def first_terms(where, fall, w_both, slabs, deep, near, start):
    rows, size, phases = slabs[0].shape
    slab_specs = [pl.BlockSpec((v.shape[0], SPAN, LANES), lambda j, h: (0, j, h)) for v in [*slabs, *deep]]
    chunk = pl.BlockSpec((rows, SPAN, LANES), lambda j, h: (0, j, h))
    local_part = pl.BlockSpec((2, rows // 2, SPAN, LANES), lambda j, h: (0, 0, start // SPAN + j, h))
    return pl.pallas_call(
        functools.partial(first_kernel, len(slabs), len(deep)),
        grid=(size // SPAN, phases // LANES),
        in_specs=[pl.BlockSpec(memory_space=pltpu.SMEM), pl.BlockSpec((2, LANES), lambda j, h: (0, h)), WHOLE]
        + slab_specs
        + [local_part] * 2,
        out_specs=[chunk] * 3,
        out_shape=[jax.ShapeDtypeStruct((rows, size, phases), F32)] * 3,
        compiler_params=PARAMS,
        cost_estimate=LIGHT,
        name="first_terms",
    )(where, fall, w_both, *slabs, *deep, *near)


def turn_kernel(swap, lifted, out):
    out[...] = swap[...] + lifted[...]


def turn(swap, lifted):
    rows, size, phases = swap.shape
    block = max(8, rows // 2)
    chunk = pl.BlockSpec((block, SPAN, phases), lambda i, j: (i, j, 0))
    return pl.pallas_call(
        turn_kernel,
        grid=(rows // block, size // SPAN),
        in_specs=[chunk, chunk],
        out_specs=chunk,
        out_shape=jax.ShapeDtypeStruct(swap.shape, F32),
        compiler_params=PARAMS,
        cost_estimate=LIGHT,
        name="turn",
    )(swap, lifted)


def finish_kernel(n_alias, _, *refs):
    out, back = refs[4 + n_alias :]
    out[...] = refs[0][...] + refs[1][...]
    back[...] = refs[2][...] + refs[3][...]


def finish(core, out, back, shape, back_size, stay, risen, start, back_at):
    rows, size, phases = stay.shape
    half = rows // 2
    steps = shape[1] // 2 // SPAN
    args, specs = [core], []
    for which in range(2):
        for array in (stay, risen):
            args.append(array)
            specs.append(pl.BlockSpec((half, SPAN, LANES), lambda j, h, c, which=which: (which, j, h)))
    alias = {}
    for n, old in enumerate((out, back)):
        if old is not None:
            alias[len(args)] = n
            args.append(old)
            specs.append(pl.BlockSpec(memory_space=pl.ANY))
    return pl.pallas_call(
        functools.partial(finish_kernel, len(alias)),
        grid_spec=pltpu.PrefetchScalarGridSpec(
            num_scalar_prefetch=1,
            grid=(size // SPAN, phases // LANES),
            in_specs=specs,
            out_specs=[
                pl.BlockSpec((half, SPAN, LANES), lambda j, h, c: (0, c[0] * steps + start // SPAN + j, h)),
                pl.BlockSpec((half, SPAN, LANES), lambda j, h, c: (0, back_at // SPAN + j, h)),
            ],
        ),
        out_shape=[jax.ShapeDtypeStruct(shape, F32), jax.ShapeDtypeStruct((half, back_size, phases), F32)],
        input_output_aliases=alias,
        compiler_params=PARAMS,
        cost_estimate=LIGHT,
        name="finish",
    )(*args)


def put_kernel(core, piece, _, out):
    out[...] = piece[...]


def put(core, out, piece, start):
    rows, size, phases = piece.shape
    steps = out.shape[1] // 2 // SPAN
    return pl.pallas_call(
        put_kernel,
        grid_spec=pltpu.PrefetchScalarGridSpec(
            num_scalar_prefetch=1,
            grid=(size // SPAN,),
            in_specs=[
                pl.BlockSpec((rows, SPAN, phases), lambda j, c: (0, j, 0)),
                pl.BlockSpec(memory_space=pl.ANY),
            ],
            out_specs=pl.BlockSpec((rows, SPAN, phases), lambda j, c: (0, c[1] * steps + start // SPAN + j, 0)),
        ),
        out_shape=jax.ShapeDtypeStruct(out.shape, F32),
        input_output_aliases={2: 0},
        compiler_params=PARAMS,
        cost_estimate=LIGHT,
        name="put",
    )(core, piece, out)


def local(occupancy, rates, increments, draw, crusher_rate, bounds):
    n_cls, n_lvl = lax.axis_size("cls"), lax.axis_size("lvl")
    occ = occupancy[0]
    rows, mid, phases = occ.shape
    half = mid // 2
    level = lax.axis_index("lvl")
    place = lax.axis_index("cls")
    k = place % 2
    core = (k, 1 - k)
    origin = [place, place ^ 1]
    for by in range(2, n_cls, 2):
        origin += [(place - by) % n_cls, ((place - by) % n_cls) ^ 1]
    where = jnp.stack([*core, level, *origin])

    def along_cls(v, by):
        return lax.ppermute(v, "cls", [(i, (i + by) % n_cls) for i in range(n_cls)])

    def other_core(v):
        return lax.ppermute(v, "cls", [(i, i ^ 1) for i in range(n_cls)])

    def two_down(v):
        return lax.ppermute(v, "lvl", [(i, i - 2) for i in range(2, n_lvl)])

    def two_up(v):
        return lax.ppermute(v, "lvl", [(i, i + 2) for i in range(1, n_lvl - 2, 2)])

    def pair_swap(v):
        return lax.ppermute(v, "lvl", [(i, i ^ 1) for i in range(n_lvl)])

    def cut(array, which, at, size):
        return lax.dynamic_slice_in_dim(array, core[which] * half + at, size, axis=1)

    chunks, groups = plan(rows, half)
    n = len(chunks)
    size = chunks[0][1]
    shifts = [2 * s for s in range(1, n_cls // 2)]
    sent = [None] * n
    tokens = []
    for lo, hi in spans(*sorted({0, n // 4, n})):
        at = chunks[lo][0]
        give = cut(occ, 1, at, (hi - lo) * size)
        if tokens:
            give, _ = gate(give, tokens[-1])
        got = other_core(give)
        tokens.append(got)
        for s in range(lo, hi):
            start = chunks[s][0]
            part = lax.slice_in_dim(got, start - at, start - at + size, axis=1)
            sent[s] = jnp.concatenate([cut(occ, 0, start, size), part], axis=0)

    far, deep = [None] * n, [None] * n

    def start_early(s):
        for by in shifts:
            straight = along_cls(cut(occ, 0, s * size, size), by)
            crossed = [(i, ((i + by) % n_cls) ^ 1) for i in range(n_cls)]
            cross = lax.ppermute(cut(occ, 1, s * size, size), "cls", crossed)
            far[s] = (far[s] or []) + [straight, cross]
        both = [(i * n_lvl + m, (i ^ 1) * n_lvl + m - 2) for i in range(n_cls) for m in range(2, n_lvl)]
        deep[s] = [two_down(cut(occ, 0, s * size, size)), lax.ppermute(cut(occ, 1, s * size, size), ("cls", "lvl"), both)]

    def start_far(s, *after):
        operand = gate(sent[s], *after)[0] if after else sent[s]
        far[s] = [along_cls(operand, by) for by in shifts]

    def start_deep(s, *after):
        operand = gate(sent[s], *after)[0] if after else sent[s]
        deep[s] = [two_down(operand)]

    start_early(0)

    a_both, *factors = prepare(where, bounds, rates, increments, draw, crusher_rate, rows)
    *factors, fall_vec = factors
    lost_a = factors.pop(4)

    parts = []

    def start_part(lo, hi, begin):
        at, span = chunks[lo][0], (hi - lo) * size
        mine, give = local_terms(where, gate(occ, begin)[0], lost_a, factors, at, span)
        return lo, hi, at, mine, give

    def send_part(part, *after):
        lo, hi, at, mine, give = part
        parts.append((lo, hi, at, (mine, other_core(gate(give, *after)[0]))))

    part = start_part(0, FIRST_ROWS, tokens[0])
    rest = start_part(FIRST_ROWS, n, part[3])
    far[0][0], _ = gate(far[0][0], rest[3])
    send_part(part, *far[0], *deep[0])
    send_part(rest, parts[0][3][1])

    out = None
    stay, rise, swap, lifted, risen = ([None] * n for _ in range(5))
    back = [None] * len(groups)
    group_of = {s: g for g, (lo, hi) in enumerate(groups) for s in range(lo, hi)}

    for s in range(n + 4):
        if s < n:
            if s >= 3:
                far[s][0], risen[s - 3] = gate(far[s][0], risen[s - 3])
            if s >= 4:
                far[s][0], out = gate(far[s][0], out)
            if s + 1 < n:
                start_far(s + 1, far[s][0])
            if s == 0:
                start_deep(1, far[0][0])
            if s + 2 < n:
                start_deep(s + 2, *deep[s])
            lo, hi, at, near = next(p for p in parts if p[0] <= s < p[1])
            stay[s], rise[s], swap[s] = first_terms(
                where, fall_vec, a_both, [sent[s]] + far[s], deep[s], near, chunks[s][0] - at
            )
            lift_me = rise[s]
            if s >= 1:
                lift_me, lifted[s - 1] = gate(lift_me, lifted[s - 1])
            lifted[s] = two_up(lift_me)
        if 1 <= s <= n:
            p = s - 1
            swap_me = turn(swap[p], lifted[p])
            if p >= 1:
                swap_me, risen[p - 1] = gate(swap_me, risen[p - 1])
            risen[p] = pair_swap(swap_me)
        if 0 <= s - 2 < n:
            p = s - 2
            g = group_of[p]
            lo, hi = groups[g]
            out, back[g] = finish(
                where, out, back[g], occ.shape, (hi - lo) * size, stay[p], risen[p], chunks[p][0], (p - lo) * size
            )
            if p == hi - 1:
                back[g] = other_core(back[g])
        if 0 <= s - 3 < n:
            p = s - 3
            lo, hi = groups[group_of[p]]
            if p == hi - 1:
                out = put(where, out, back[group_of[p]], chunks[lo][0])
    return out[None]


def solution(mesh):
    in_specs = (P("lvl", "cls", None, None), P(), P(), P(), P(), P())
    out_specs = P("lvl", "cls", None, None)
    return jax.shard_map(local, mesh=mesh, in_specs=in_specs, out_specs=out_specs, check_vma=False)
```

```python
import functools

import jax
import jax.numpy as jnp
from jax import lax
from jax.experimental import pallas as pl
from jax.experimental.pallas import tpu as pltpu
from jax.sharding import PartitionSpec as P

F32 = jnp.float32
BF16 = jnp.bfloat16
VMEM_LIMIT = 56 * 2**20
SPAN, LANES = 8, 128
FIRST_ROWS = 2
LIGHT = pl.CostEstimate(flops=1000, transcendentals=0, bytes_accessed=1000)
PARAMS = pltpu.CompilerParams(vmem_limit_bytes=VMEM_LIMIT)
WHOLE = pl.BlockSpec(memory_space=pltpu.VMEM)


def gate(*values):
    return lax.optimization_barrier(values)


def flag(cond):
    return jnp.where(cond, 1.0, 0.0).astype(F32)


def halves(x):
    high = x.astype(BF16)
    low = (x - high.astype(F32)).astype(BF16)
    return high, low


def halves_outside(x):
    high = lax.reduce_precision(x, 8, 7)
    return high.astype(BF16), (x - high).astype(BF16)


def dot(a, b):
    return jnp.dot(a, b, preferred_element_type=F32)


def plan(rows, length):
    n = max(4, rows // 4)
    size = length // n
    chunks = [(s * size, size) for s in range(n)]
    return chunks, [(0, n - 2), (n - 2, n - 1), (n - 1, n)]


def spans(*bounds):
    return list(zip(bounds[:-1], bounds[1:]))


def prepare_kernel(rows, where, bounds, rates, inc_rows, inc_cols, draw, crusher, a_out, c_hi, c_lo, b_hi, b_lo, lost_a, lost_b,
                   left_c, fall, flip):
    level = where[2]
    top, bottom = bounds[1], bounds[0]
    phases = rates.shape[1]
    totals = [jnp.sum(rates[c], axis=1, keepdims=True) for c in range(3)]
    uniform = jnp.max(crusher[...], axis=1, keepdims=True)
    for total in totals:
        uniform = uniform + jnp.max(total, axis=0, keepdims=True)
    scale = 1.0 / uniform
    rise_ok = jnp.where(level + 1 <= top, 1.0, 0.0)

    def opened(inc):
        return jnp.where((inc == 0) | (level + inc <= top), 1.0, 0.0)

    def masks(inc):
        return [jnp.where(inc == 0, 1.0, 0.0) * scale, jnp.where(inc == 1, 1.0, 0.0) * (rise_ok * scale)]

    lost_a[...] = totals[0] * opened(inc_cols[0]) * scale
    lost_b[...] = totals[1] * opened(inc_cols[1]) * scale
    total_c = jnp.sum(jnp.transpose(rates[2]), axis=0, keepdims=True)
    here = crusher[...] * jnp.where(level - draw[...] >= bottom, 1.0, 0.0)
    deep = crusher[...] * jnp.where(level + 2 - draw[...] >= bottom, 1.0, 0.0)
    left_c[...] = 1.0 - total_c * opened(inc_rows[2:3]) * scale - here * scale
    fall[0:1] = jnp.where(level % 2 == 0, deep, here) * jnp.where(draw[...] == 1, 1.0, 0.0) * scale
    fall[1:2] = deep * jnp.where(draw[...] == 2, 1.0, 0.0) * scale
    for n, mask in enumerate(masks(inc_cols[2])):
        high, low = halves(rates[2] * mask)
        c_hi[:, n * phases : (n + 1) * phases] = high
        c_lo[:, n * phases : (n + 1) * phases] = low
    for n, mask in enumerate(masks(inc_cols[1])):
        high, low = halves(jnp.transpose(rates[1] * mask))
        b_hi[n] = high
        b_lo[n] = low
    spots = [pl.ds(pl.multiple_of(where[3 + n] * rows, 8), rows) for n in range(phases // rows)]
    ordered = jnp.concatenate([rates[0, spot] for spot in spots], axis=0)
    inc = jnp.concatenate([inc_cols[0, spot] for spot in spots], axis=0)
    for n, mask in enumerate(masks(inc)):
        flip[...] = jnp.transpose(ordered * mask)
        for which in range(2):
            at = (2 * n + which) * rows
            high, low = halves(flip[spots[which]])
            a_out[at : at + rows] = high
            a_out[4 * rows + at : 5 * rows + at] = low


def prepare(where, bounds, rates, increments, draw, crusher_rate, rows):
    phases = rates.shape[1]
    smem = pl.BlockSpec(memory_space=pltpu.SMEM)
    shapes = [
        ((8 * rows, phases), BF16),
        ((phases, 2 * phases), BF16),
        ((phases, 2 * phases), BF16),
        ((2, phases, phases), BF16),
        ((2, phases, phases), BF16),
        ((phases, 1), F32),
        ((phases, 1), F32),
        ((1, phases), F32),
        ((2, phases), F32),
    ]
    return pl.pallas_call(
        functools.partial(prepare_kernel, rows),
        in_specs=[smem, smem] + [WHOLE] * 5,
        out_specs=[WHOLE] * len(shapes),
        out_shape=[jax.ShapeDtypeStruct(*v) for v in shapes],
        scratch_shapes=[pltpu.VMEM((phases, phases), F32)],
        compiler_params=PARAMS,
        cost_estimate=LIGHT,
        name="prepare",
    )(where, bounds, rates, increments, increments[:, :, None], draw[None], crusher_rate[None])


def local_kernel(at, half, where, lost_a, occ, c_hi, c_lo, b_hi, b_lo, lost_b, left_c, mine, peer, b_both, left_b):
    block, phases = occ.shape[0], occ.shape[2]
    size = mine.shape[2]
    rows = [pl.ds(pl.multiple_of(where[n] * half + at, 16), size) for n in range(2)]

    @pl.when(pl.program_id(0) == 0)
    def _():
        for n in range(2):
            left_b[n * size : (n + 1) * size] = lost_b[rows[n]]
            for m in range(2):
                spot = (2 * m + n) * size
                b_both[spot : spot + size] = b_hi[m, rows[n]]
                b_both[4 * size + spot : 5 * size + spot] = b_lo[m, rows[n]]

    first = where[3] * (pl.num_programs(0) * block) + pl.program_id(0) * block
    y = jnp.concatenate([occ[i, r] for i in range(block) for r in rows], axis=0)
    y_hi, y_lo = halves(y)
    n_y = y.shape[0]
    by_c = dot(jnp.concatenate([y_hi, y_lo], axis=0), c_hi[...])
    by_c = by_c[:n_y] + by_c[n_y:] + dot(y_hi, c_lo[...])
    for i in range(block):
        x_hi, x_lo = halves(occ[i])
        by_b = dot(b_both[...], x_hi)
        by_b = by_b[: 4 * size] + by_b[4 * size :] + dot(b_both[: 4 * size], x_lo)
        here = slice(2 * size * i, 2 * size * (i + 1))
        left = left_c[...] - lost_a[pl.ds(first + i, 1)] - left_b[...]
        base = by_c[here, :phases] + by_b[: 2 * size] + y[here] * left
        rise = by_c[here, phases:] + by_b[2 * size :]
        for n, value in enumerate((base, rise)):
            mine[n, i] = value[:size]
            peer[n, i] = value[size:]


def local_terms(where, occ, lost_a, factors, at, size):
    rows, mid, phases = occ.shape
    block = 8
    out = pl.BlockSpec((2, block, size, phases), lambda i, c: (0, i, 0, 0))
    return pl.pallas_call(
        functools.partial(local_kernel, at, mid // 2),
        grid_spec=pltpu.PrefetchScalarGridSpec(
            num_scalar_prefetch=1,
            grid=(rows // block,),
            in_specs=[WHOLE, pl.BlockSpec((block, mid, phases), lambda i, c: (i, 0, 0))] + [WHOLE] * len(factors),
            out_specs=[out] * 2,
            scratch_shapes=[pltpu.VMEM((8 * size, mid), BF16), pltpu.VMEM((2 * size, 1), F32)],
        ),
        out_shape=[jax.ShapeDtypeStruct((2, rows, size, phases), F32)] * 2,
        compiler_params=PARAMS,
        cost_estimate=LIGHT,
        name="local_terms",
    )(where, lost_a, occ, *factors)


def first_kernel(n_slabs, n_deep, where, fall, *refs):
    w_both = refs[0]
    slabs = refs[1 : 1 + n_slabs]
    deep = refs[1 + n_slabs : 1 + n_slabs + n_deep]
    mine, peer, stay_out, rise_out, swap_out = refs[1 + n_slabs + n_deep :]
    rows, span, lanes = stay_out.shape
    flat = [ref.reshape(ref.shape[0] * span, lanes) for ref in slabs]
    stay_flat = stay_out.reshape(rows * span, lanes)
    rise_flat = rise_out.reshape(rows * span, lanes)
    for b in range(0, span, 2):
        ats = [pl.ds(b, rows, stride=span), pl.ds(b + 1, rows, stride=span)]
        parts = []
        for ref in flat:
            picks = [pl.ds(b + n, ref.shape[0] // span, stride=span) for n in range(2)]
            parts.append(halves(jnp.concatenate([ref[pick, :] for pick in picks], axis=1)))
        g_hi = jnp.concatenate([p[0] for p in parts], axis=0)
        g_lo = jnp.concatenate([p[1] for p in parts], axis=0)
        both = dot(w_both[...], g_hi)
        out = both[: 2 * rows] + both[2 * rows :] + dot(w_both[: 2 * rows], g_lo)
        for n, at in enumerate(ats):
            stay_flat[at, :] = out[:rows, n * lanes : (n + 1) * lanes]
            rise_flat[at, :] = out[rows:, n * lanes : (n + 1) * lanes]
    half = rows // 2
    once, twice = fall[0:1], fall[1:2]
    for which, near in enumerate((mine, peer)):
        part = slice(which * half, (which + 1) * half)
        far_down = deep[which][...] if n_deep == 2 else deep[0][part]
        stay_out[part] += near[0] + far_down * twice
        lift = rise_out[part] + near[1]
        rise_out[part] = lift

        @pl.when(where[2] % 2 == 0)
        def _():
            swap_out[part] = lift + far_down * once

    @pl.when(where[2] % 2 != 0)
    def _():
        at = 0
        for ref in slabs:
            if at < rows:
                swap_out[at : at + ref.shape[0]] = ref[...] * once
            at += ref.shape[0]


def first_terms(where, fall, w_both, slabs, deep, near, start):
    rows, size, phases = slabs[0].shape
    slab_specs = [pl.BlockSpec((v.shape[0], SPAN, LANES), lambda j, h: (0, j, h)) for v in [*slabs, *deep]]
    chunk = pl.BlockSpec((rows, SPAN, LANES), lambda j, h: (0, j, h))
    local_part = pl.BlockSpec((2, rows // 2, SPAN, LANES), lambda j, h: (0, 0, start // SPAN + j, h))
    return pl.pallas_call(
        functools.partial(first_kernel, len(slabs), len(deep)),
        grid=(size // SPAN, phases // LANES),
        in_specs=[pl.BlockSpec(memory_space=pltpu.SMEM), pl.BlockSpec((2, LANES), lambda j, h: (0, h)), WHOLE]
        + slab_specs
        + [local_part] * 2,
        out_specs=[chunk] * 3,
        out_shape=[jax.ShapeDtypeStruct((rows, size, phases), F32)] * 3,
        compiler_params=PARAMS,
        cost_estimate=LIGHT,
        name="first_terms",
    )(where, fall, w_both, *slabs, *deep, *near)


def turn_kernel(swap, lifted, out):
    out[...] = swap[...] + lifted[...]


def turn(swap, lifted):
    rows, size, phases = swap.shape
    block = max(8, rows // 2)
    chunk = pl.BlockSpec((block, SPAN, phases), lambda i, j: (i, j, 0))
    return pl.pallas_call(
        turn_kernel,
        grid=(rows // block, size // SPAN),
        in_specs=[chunk, chunk],
        out_specs=chunk,
        out_shape=jax.ShapeDtypeStruct(swap.shape, F32),
        compiler_params=PARAMS,
        cost_estimate=LIGHT,
        name="turn",
    )(swap, lifted)


def finish_kernel(n_alias, _, *refs):
    out, back = refs[4 + n_alias :]
    out[...] = refs[0][...] + refs[1][...]
    back[...] = refs[2][...] + refs[3][...]


def finish(core, out, back, shape, back_size, stay, risen, start, back_at):
    rows, size, phases = stay.shape
    half = rows // 2
    steps = shape[1] // 2 // SPAN
    args, specs = [core], []
    for which in range(2):
        for array in (stay, risen):
            args.append(array)
            specs.append(pl.BlockSpec((half, SPAN, LANES), lambda j, h, c, which=which: (which, j, h)))
    alias = {}
    for n, old in enumerate((out, back)):
        if old is not None:
            alias[len(args)] = n
            args.append(old)
            specs.append(pl.BlockSpec(memory_space=pl.ANY))
    return pl.pallas_call(
        functools.partial(finish_kernel, len(alias)),
        grid_spec=pltpu.PrefetchScalarGridSpec(
            num_scalar_prefetch=1,
            grid=(size // SPAN, phases // LANES),
            in_specs=specs,
            out_specs=[
                pl.BlockSpec((half, SPAN, LANES), lambda j, h, c: (0, c[0] * steps + start // SPAN + j, h)),
                pl.BlockSpec((half, SPAN, LANES), lambda j, h, c: (0, back_at // SPAN + j, h)),
            ],
        ),
        out_shape=[jax.ShapeDtypeStruct(shape, F32), jax.ShapeDtypeStruct((half, back_size, phases), F32)],
        input_output_aliases=alias,
        compiler_params=PARAMS,
        cost_estimate=LIGHT,
        name="finish",
    )(*args)


def put_kernel(core, piece, _, out):
    out[...] = piece[...]


def put(core, out, piece, start):
    rows, size, phases = piece.shape
    steps = out.shape[1] // 2 // SPAN
    return pl.pallas_call(
        put_kernel,
        grid_spec=pltpu.PrefetchScalarGridSpec(
            num_scalar_prefetch=1,
            grid=(size // SPAN,),
            in_specs=[
                pl.BlockSpec((rows, SPAN, phases), lambda j, c: (0, j, 0)),
                pl.BlockSpec(memory_space=pl.ANY),
            ],
            out_specs=pl.BlockSpec((rows, SPAN, phases), lambda j, c: (0, c[1] * steps + start // SPAN + j, 0)),
        ),
        out_shape=jax.ShapeDtypeStruct(out.shape, F32),
        input_output_aliases={2: 0},
        compiler_params=PARAMS,
        cost_estimate=LIGHT,
        name="put",
    )(core, piece, out)


def local(occupancy, rates, increments, draw, crusher_rate, bounds):
    n_cls, n_lvl = lax.axis_size("cls"), lax.axis_size("lvl")
    occ = occupancy[0]
    rows, mid, phases = occ.shape
    half = mid // 2
    level = lax.axis_index("lvl")
    place = lax.axis_index("cls")
    k = place % 2
    core = (k, 1 - k)
    origin = [place, place ^ 1]
    for by in range(2, n_cls, 2):
        origin += [(place - by) % n_cls, ((place - by) % n_cls) ^ 1]
    where = jnp.stack([*core, level, *origin])

    def along_cls(v, by):
        return lax.ppermute(v, "cls", [(i, (i + by) % n_cls) for i in range(n_cls)])

    def other_core(v):
        return lax.ppermute(v, "cls", [(i, i ^ 1) for i in range(n_cls)])

    def two_down(v):
        return lax.ppermute(v, "lvl", [(i, i - 2) for i in range(2, n_lvl)])

    def two_up(v):
        return lax.ppermute(v, "lvl", [(i, i + 2) for i in range(1, n_lvl - 2, 2)])

    def pair_swap(v):
        return lax.ppermute(v, "lvl", [(i, i ^ 1) for i in range(n_lvl)])

    def cut(array, which, at, size):
        return lax.dynamic_slice_in_dim(array, core[which] * half + at, size, axis=1)

    chunks, groups = plan(rows, half)
    n = len(chunks)
    size = chunks[0][1]
    shifts = [2 * s for s in range(1, n_cls // 2)]
    sent = [None] * n
    tokens, gives = [], []
    for lo, hi in spans(*sorted({0, n // 4, n})):
        at = chunks[lo][0]
        give = cut(occ, 1, at, (hi - lo) * size)
        if tokens:
            give, _ = gate(give, sent[0])
        gives.append(give)
        got = other_core(give)
        tokens.append(got)
        for s in range(lo, hi):
            start = chunks[s][0]
            part = lax.slice_in_dim(got, start - at, start - at + size, axis=1)
            sent[s] = jnp.concatenate([cut(occ, 0, start, size), part], axis=0)

    far, deep = [None] * n, [None] * n

    def start_early(s):
        for by in shifts:
            straight = along_cls(cut(occ, 0, s * size, size), by)
            crossed = [(i, ((i + by) % n_cls) ^ 1) for i in range(n_cls)]
            cross = lax.ppermute(cut(occ, 1, s * size, size), "cls", crossed)
            far[s] = (far[s] or []) + [straight, cross]
        both = [(i * n_lvl + m, (i ^ 1) * n_lvl + m - 2) for i in range(n_cls) for m in range(2, n_lvl)]
        deep[s] = [two_down(cut(occ, 0, s * size, size)), lax.ppermute(cut(occ, 1, s * size, size), ("cls", "lvl"), both)]

    def start_far(s, *after):
        operand = gate(sent[s], *after)[0] if after else sent[s]
        far[s] = [along_cls(operand, by) for by in shifts]

    def start_deep(s, *after):
        operand = gate(sent[s], *after)[0] if after else sent[s]
        deep[s] = [two_down(operand)]

    start_early(0)

    a_both, *factors = prepare(where, bounds, rates, increments, draw, crusher_rate, rows)
    *factors, fall_vec = factors
    lost_a = factors.pop(4)

    parts = []

    def start_part(lo, hi, *begin):
        at, span = chunks[lo][0], (hi - lo) * size
        mine, give = local_terms(where, gate(occ, *begin)[0], lost_a, factors, at, span)
        return lo, hi, at, mine, give

    def send_part(part, *after):
        lo, hi, at, mine, give = part
        parts.append((lo, hi, at, (mine, other_core(gate(give, *after)[0]))))

    part = start_part(0, FIRST_ROWS, tokens[0])
    rest = start_part(FIRST_ROWS, n, part[3], gives[1], sent[0], sent[1])
    far[0][0], _ = gate(far[0][0], rest[3])
    send_part(part, *far[0], *deep[0])
    send_part(rest, parts[0][3][1])

    out = None
    stay, rise, swap, lifted, risen = ([None] * n for _ in range(5))
    back = [None] * len(groups)
    group_of = {s: g for g, (lo, hi) in enumerate(groups) for s in range(lo, hi)}

    for s in range(n + 4):
        if s < n:
            if s >= 3:
                far[s][0], risen[s - 3] = gate(far[s][0], risen[s - 3])
            if s >= 4:
                far[s][0], out = gate(far[s][0], out)
            if s + 1 < n:
                start_far(s + 1, far[s][0])
            if s == 0:
                start_deep(1, far[0][0])
            if s + 2 < n:
                start_deep(s + 2, *deep[s])
            lo, hi, at, near = next(p for p in parts if p[0] <= s < p[1])
            stay[s], rise[s], swap[s] = first_terms(
                where, fall_vec, a_both, [sent[s]] + far[s], deep[s], near, chunks[s][0] - at
            )
            lift_me = rise[s]
            if s >= 1:
                lift_me, lifted[s - 1] = gate(lift_me, lifted[s - 1])
            lifted[s] = two_up(lift_me)
        if 1 <= s <= n:
            p = s - 1
            swap_me = turn(swap[p], lifted[p])
            if p >= 1:
                swap_me, risen[p - 1] = gate(swap_me, risen[p - 1])
            risen[p] = pair_swap(swap_me)
        if 0 <= s - 2 < n:
            p = s - 2
            g = group_of[p]
            lo, hi = groups[g]
            out, back[g] = finish(
                where, out, back[g], occ.shape, (hi - lo) * size, stay[p], risen[p], chunks[p][0], (p - lo) * size
            )
            if p == hi - 1:
                back[g] = other_core(back[g])
        if 0 <= s - 3 < n:
            p = s - 3
            lo, hi = groups[group_of[p]]
            if p == hi - 1:
                out = put(where, out, back[group_of[p]], chunks[lo][0])
    return out[None]


def solution(mesh):
    in_specs = (P("lvl", "cls", None, None), P(), P(), P(), P(), P())
    out_specs = P("lvl", "cls", None, None)
    return jax.shard_map(local, mesh=mesh, in_specs=in_specs, out_specs=out_specs, check_vma=False)
```

```python
import functools

import jax
import jax.numpy as jnp
from jax import lax
from jax.experimental import pallas as pl
from jax.experimental.pallas import tpu as pltpu
from jax.sharding import PartitionSpec as P

F32 = jnp.float32
BF16 = jnp.bfloat16
VMEM_LIMIT = 56 * 2**20
SPAN, LANES = 8, 128
LIGHT = pl.CostEstimate(flops=1000, transcendentals=0, bytes_accessed=1000)
PARAMS = pltpu.CompilerParams(vmem_limit_bytes=VMEM_LIMIT)
WHOLE = pl.BlockSpec(memory_space=pltpu.VMEM)


def gate(*values):
    return lax.optimization_barrier(values)


def flag(cond):
    return jnp.where(cond, 1.0, 0.0).astype(F32)


def halves(x):
    high = x.astype(BF16)
    low = (x - high.astype(F32)).astype(BF16)
    return high, low


def halves_outside(x):
    high = lax.reduce_precision(x, 8, 7)
    return high.astype(BF16), (x - high).astype(BF16)


def dot(a, b):
    return jnp.dot(a, b, preferred_element_type=F32)


def plan(rows, length):
    n = max(4, rows // 4)
    size = length // n
    chunks = [(s * size, size) for s in range(n)]
    return chunks, [(0, n - 2), (n - 2, n - 1), (n - 1, n)]


def spans(*bounds):
    return list(zip(bounds[:-1], bounds[1:]))


def prepare_kernel(rows, where, bounds, rates, inc_rows, inc_cols, draw, crusher, a_out, c_hi, c_lo, b_hi, b_lo, lost_a, lost_b,
                   left_c, fall, flip):
    level = where[2]
    top, bottom = bounds[1], bounds[0]
    phases = rates.shape[1]
    totals = [jnp.sum(rates[c], axis=1, keepdims=True) for c in range(3)]
    uniform = jnp.max(crusher[...], axis=1, keepdims=True)
    for total in totals:
        uniform = uniform + jnp.max(total, axis=0, keepdims=True)
    scale = 1.0 / uniform
    rise_ok = jnp.where(level + 1 <= top, 1.0, 0.0)

    def opened(inc):
        return jnp.where((inc == 0) | (level + inc <= top), 1.0, 0.0)

    def masks(inc):
        return [jnp.where(inc == 0, 1.0, 0.0) * scale, jnp.where(inc == 1, 1.0, 0.0) * (rise_ok * scale)]

    lost_a[...] = totals[0] * opened(inc_cols[0]) * scale
    lost_b[...] = totals[1] * opened(inc_cols[1]) * scale
    total_c = jnp.sum(jnp.transpose(rates[2]), axis=0, keepdims=True)
    here = crusher[...] * jnp.where(level - draw[...] >= bottom, 1.0, 0.0)
    deep = crusher[...] * jnp.where(level + 2 - draw[...] >= bottom, 1.0, 0.0)
    left_c[...] = 1.0 - total_c * opened(inc_rows[2:3]) * scale - here * scale
    fall[0:1] = jnp.where(level % 2 == 0, deep, here) * jnp.where(draw[...] == 1, 1.0, 0.0) * scale
    fall[1:2] = deep * jnp.where(draw[...] == 2, 1.0, 0.0) * scale
    for n, mask in enumerate(masks(inc_cols[2])):
        high, low = halves(rates[2] * mask)
        c_hi[:, n * phases : (n + 1) * phases] = high
        c_lo[:, n * phases : (n + 1) * phases] = low
    for n, mask in enumerate(masks(inc_cols[1])):
        high, low = halves(jnp.transpose(rates[1] * mask))
        b_hi[n] = high
        b_lo[n] = low
    spots = [pl.ds(pl.multiple_of(where[3 + n] * rows, 8), rows) for n in range(phases // rows)]
    ordered = jnp.concatenate([rates[0, spot] for spot in spots], axis=0)
    inc = jnp.concatenate([inc_cols[0, spot] for spot in spots], axis=0)
    for n, mask in enumerate(masks(inc)):
        flip[...] = jnp.transpose(ordered * mask)
        for which in range(2):
            at = (2 * n + which) * rows
            high, low = halves(flip[spots[which]])
            a_out[at : at + rows] = high
            a_out[4 * rows + at : 5 * rows + at] = low


def prepare(where, bounds, rates, increments, draw, crusher_rate, rows):
    phases = rates.shape[1]
    smem = pl.BlockSpec(memory_space=pltpu.SMEM)
    shapes = [
        ((8 * rows, phases), BF16),
        ((phases, 2 * phases), BF16),
        ((phases, 2 * phases), BF16),
        ((2, phases, phases), BF16),
        ((2, phases, phases), BF16),
        ((phases, 1), F32),
        ((phases, 1), F32),
        ((1, phases), F32),
        ((2, phases), F32),
    ]
    return pl.pallas_call(
        functools.partial(prepare_kernel, rows),
        in_specs=[smem, smem] + [WHOLE] * 5,
        out_specs=[WHOLE] * len(shapes),
        out_shape=[jax.ShapeDtypeStruct(*v) for v in shapes],
        scratch_shapes=[pltpu.VMEM((phases, phases), F32)],
        compiler_params=PARAMS,
        cost_estimate=LIGHT,
        name="prepare",
    )(where, bounds, rates, increments, increments[:, :, None], draw[None], crusher_rate[None])


def local_kernel(half, where, lost_a, occ, c_hi, c_lo, b_hi, b_lo, lost_b, left_c, *outs):
    block, phases = occ.shape[0], occ.shape[2]
    mine, peer, mine_rest, peer_rest, b_both, left_b = outs
    size, cut = half, mine.shape[2]
    rows = [pl.ds(pl.multiple_of(where[n] * half, 16), size) for n in range(2)]

    @pl.when(pl.program_id(0) == 0)
    def _():
        for n in range(2):
            left_b[n * size : (n + 1) * size] = lost_b[rows[n]]
            for m in range(2):
                spot = (2 * m + n) * size
                b_both[spot : spot + size] = b_hi[m, rows[n]]
                b_both[4 * size + spot : 5 * size + spot] = b_lo[m, rows[n]]

    first = where[3] * (pl.num_programs(0) * block) + pl.program_id(0) * block
    y = jnp.concatenate([occ[i, r] for i in range(block) for r in rows], axis=0)
    y_hi, y_lo = halves(y)
    n_y = y.shape[0]
    by_c = dot(jnp.concatenate([y_hi, y_lo], axis=0), c_hi[...])
    by_c = by_c[:n_y] + by_c[n_y:] + dot(y_hi, c_lo[...])
    for i in range(block):
        x_hi, x_lo = halves(occ[i])
        by_b = dot(b_both[...], x_hi)
        by_b = by_b[: 4 * size] + by_b[4 * size :] + dot(b_both[: 4 * size], x_lo)
        here = slice(2 * size * i, 2 * size * (i + 1))
        left = left_c[...] - lost_a[pl.ds(first + i, 1)] - left_b[...]
        base = by_c[here, :phases] + by_b[: 2 * size] + y[here] * left
        rise = by_c[here, phases:] + by_b[2 * size :]
        for n, value in enumerate((base, rise)):
            mine[n, i] = value[:cut]
            mine_rest[n, i] = value[cut:size]
            peer[n, i] = value[size : size + cut]
            peer_rest[n, i] = value[size + cut :]


def local_terms(where, occ, lost_a, factors, first):
    rows, mid, phases = occ.shape
    block, size = 8, mid // 2
    sizes = [first, first, size - first, size - first]
    return pl.pallas_call(
        functools.partial(local_kernel, size),
        grid_spec=pltpu.PrefetchScalarGridSpec(
            num_scalar_prefetch=1,
            grid=(rows // block,),
            in_specs=[WHOLE, pl.BlockSpec((block, mid, phases), lambda i, c: (i, 0, 0))] + [WHOLE] * len(factors),
            out_specs=[pl.BlockSpec((2, block, v, phases), lambda i, c: (0, i, 0, 0)) for v in sizes],
            scratch_shapes=[pltpu.VMEM((8 * size, mid), BF16), pltpu.VMEM((2 * size, 1), F32)],
        ),
        out_shape=[jax.ShapeDtypeStruct((2, rows, v, phases), F32) for v in sizes],
        compiler_params=PARAMS,
        cost_estimate=LIGHT,
        name="local_terms",
    )(where, lost_a, occ, *factors)


def first_kernel(n_slabs, n_deep, where, fall, *refs):
    w_both = refs[0]
    slabs = refs[1 : 1 + n_slabs]
    deep = refs[1 + n_slabs : 1 + n_slabs + n_deep]
    mine, peer, stay_out, rise_out, swap_out = refs[1 + n_slabs + n_deep :]
    rows, span, lanes = stay_out.shape
    flat = [ref.reshape(ref.shape[0] * span, lanes) for ref in slabs]
    stay_flat = stay_out.reshape(rows * span, lanes)
    rise_flat = rise_out.reshape(rows * span, lanes)
    for b in range(0, span, 2):
        ats = [pl.ds(b, rows, stride=span), pl.ds(b + 1, rows, stride=span)]
        parts = []
        for ref in flat:
            picks = [pl.ds(b + n, ref.shape[0] // span, stride=span) for n in range(2)]
            parts.append(halves(jnp.concatenate([ref[pick, :] for pick in picks], axis=1)))
        g_hi = jnp.concatenate([p[0] for p in parts], axis=0)
        g_lo = jnp.concatenate([p[1] for p in parts], axis=0)
        both = dot(w_both[...], g_hi)
        out = both[: 2 * rows] + both[2 * rows :] + dot(w_both[: 2 * rows], g_lo)
        for n, at in enumerate(ats):
            stay_flat[at, :] = out[:rows, n * lanes : (n + 1) * lanes]
            rise_flat[at, :] = out[rows:, n * lanes : (n + 1) * lanes]
    half = rows // 2
    once, twice = fall[0:1], fall[1:2]
    for which, near in enumerate((mine, peer)):
        part = slice(which * half, (which + 1) * half)
        far_down = deep[which][...] if n_deep == 2 else deep[0][part]
        stay_out[part] += near[0] + far_down * twice
        lift = rise_out[part] + near[1]
        rise_out[part] = lift

        @pl.when(where[2] % 2 == 0)
        def _():
            swap_out[part] = lift + far_down * once

    @pl.when(where[2] % 2 != 0)
    def _():
        at = 0
        for ref in slabs:
            if at < rows:
                swap_out[at : at + ref.shape[0]] = ref[...] * once
            at += ref.shape[0]


def first_terms(where, fall, w_both, slabs, deep, near, start, size):
    rows, _, phases = slabs[0][0].shape
    slab_specs = [
        pl.BlockSpec((v.shape[0], SPAN, LANES), lambda j, h, at=at: (0, at // SPAN + j, h)) for v, at in [*slabs, *deep]
    ]
    chunk = pl.BlockSpec((rows, SPAN, LANES), lambda j, h: (0, j, h))
    local_part = pl.BlockSpec((2, rows // 2, SPAN, LANES), lambda j, h: (0, 0, start // SPAN + j, h))
    return pl.pallas_call(
        functools.partial(first_kernel, len(slabs), len(deep)),
        grid=(size // SPAN, phases // LANES),
        in_specs=[pl.BlockSpec(memory_space=pltpu.SMEM), pl.BlockSpec((2, LANES), lambda j, h: (0, h)), WHOLE]
        + slab_specs
        + [local_part] * 2,
        out_specs=[chunk] * 3,
        out_shape=[jax.ShapeDtypeStruct((rows, size, phases), F32)] * 3,
        compiler_params=PARAMS,
        cost_estimate=LIGHT,
        name="first_terms",
    )(where, fall, w_both, *[v for v, _ in [*slabs, *deep]], *near)


def turn_kernel(swap, lifted, out):
    out[...] = swap[...] + lifted[...]


def turn(swap, lifted):
    rows, size, phases = swap.shape
    block = max(8, rows // 2)
    chunk = pl.BlockSpec((block, SPAN, phases), lambda i, j: (i, j, 0))
    return pl.pallas_call(
        turn_kernel,
        grid=(rows // block, size // SPAN),
        in_specs=[chunk, chunk],
        out_specs=chunk,
        out_shape=jax.ShapeDtypeStruct(swap.shape, F32),
        compiler_params=PARAMS,
        cost_estimate=LIGHT,
        name="turn",
    )(swap, lifted)


def finish_kernel(n_alias, _, *refs):
    out, back = refs[4 + n_alias :]
    out[...] = refs[0][...] + refs[1][...]
    back[...] = refs[2][...] + refs[3][...]


def finish(core, out, back, shape, back_size, stay, risen, start, back_at):
    rows, size, phases = stay.shape
    half = rows // 2
    steps = shape[1] // 2 // SPAN
    args, specs = [core], []
    for which in range(2):
        for array in (stay, risen):
            args.append(array)
            specs.append(pl.BlockSpec((half, SPAN, LANES), lambda j, h, c, which=which: (which, j, h)))
    alias = {}
    for n, old in enumerate((out, back)):
        if old is not None:
            alias[len(args)] = n
            args.append(old)
            specs.append(pl.BlockSpec(memory_space=pl.ANY))
    return pl.pallas_call(
        functools.partial(finish_kernel, len(alias)),
        grid_spec=pltpu.PrefetchScalarGridSpec(
            num_scalar_prefetch=1,
            grid=(size // SPAN, phases // LANES),
            in_specs=specs,
            out_specs=[
                pl.BlockSpec((half, SPAN, LANES), lambda j, h, c: (0, c[0] * steps + start // SPAN + j, h)),
                pl.BlockSpec((half, SPAN, LANES), lambda j, h, c: (0, back_at // SPAN + j, h)),
            ],
        ),
        out_shape=[jax.ShapeDtypeStruct(shape, F32), jax.ShapeDtypeStruct((half, back_size, phases), F32)],
        input_output_aliases=alias,
        compiler_params=PARAMS,
        cost_estimate=LIGHT,
        name="finish",
    )(*args)


def put_kernel(core, piece, _, out):
    out[...] = piece[...]


def put(core, out, piece, start):
    rows, size, phases = piece.shape
    steps = out.shape[1] // 2 // SPAN
    return pl.pallas_call(
        put_kernel,
        grid_spec=pltpu.PrefetchScalarGridSpec(
            num_scalar_prefetch=1,
            grid=(size // SPAN,),
            in_specs=[
                pl.BlockSpec((rows, SPAN, phases), lambda j, c: (0, j, 0)),
                pl.BlockSpec(memory_space=pl.ANY),
            ],
            out_specs=pl.BlockSpec((rows, SPAN, phases), lambda j, c: (0, c[1] * steps + start // SPAN + j, 0)),
        ),
        out_shape=jax.ShapeDtypeStruct(out.shape, F32),
        input_output_aliases={2: 0},
        compiler_params=PARAMS,
        cost_estimate=LIGHT,
        name="put",
    )(core, piece, out)


def local(occupancy, rates, increments, draw, crusher_rate, bounds):
    n_cls, n_lvl = lax.axis_size("cls"), lax.axis_size("lvl")
    occ = occupancy[0]
    rows, mid, phases = occ.shape
    half = mid // 2
    level = lax.axis_index("lvl")
    place = lax.axis_index("cls")
    k = place % 2
    core = (k, 1 - k)
    origin = [place, place ^ 1]
    for by in range(2, n_cls, 2):
        origin += [(place - by) % n_cls, ((place - by) % n_cls) ^ 1]
    where = jnp.stack([*core, level, *origin])

    def along_cls(v, by):
        return lax.ppermute(v, "cls", [(i, (i + by) % n_cls) for i in range(n_cls)])

    def other_core(v):
        return lax.ppermute(v, "cls", [(i, i ^ 1) for i in range(n_cls)])

    def two_down(v):
        return lax.ppermute(v, "lvl", [(i, i - 2) for i in range(2, n_lvl)])

    def two_up(v):
        return lax.ppermute(v, "lvl", [(i, i + 2) for i in range(1, n_lvl - 2, 2)])

    def pair_swap(v):
        return lax.ppermute(v, "lvl", [(i, i ^ 1) for i in range(n_lvl)])

    def cut(array, which, at, size):
        return lax.dynamic_slice_in_dim(array, core[which] * half + at, size, axis=1)

    chunks, groups = plan(rows, half)
    n = len(chunks)
    size = chunks[0][1]
    shifts = [2 * s for s in range(1, n_cls // 2)]
    sent = [None] * n

    def exchange(lo, hi, *after):
        at = chunks[lo][0]
        give = cut(occ, 1, at, (hi - lo) * size)
        if after:
            give = gate(give, *after)[0]
        got = other_core(give)
        for s in range(lo, hi):
            start = chunks[s][0]
            part = lax.slice_in_dim(got, start - at, start - at + size, axis=1)
            sent[s] = jnp.concatenate([cut(occ, 0, start, size), part], axis=0)
        return give, got

    quarter = max(3, n // 4)
    _, token = exchange(0, quarter)

    far, deep = [None] * n, [None] * n

    def start_early():
        own, other = cut(occ, 0, 0, 2 * size), cut(occ, 1, 0, 2 * size)
        got = []
        for by in shifts:
            crossed = [(i, ((i + by) % n_cls) ^ 1) for i in range(n_cls)]
            got += [along_cls(own, by), lax.ppermute(other, "cls", crossed)]
        far[0], far[1] = list(got), list(got)
        both = [(i * n_lvl + m, (i ^ 1) * n_lvl + m - 2) for i in range(n_cls) for m in range(2, n_lvl)]
        got = [two_down(own), lax.ppermute(other, ("cls", "lvl"), both)]
        deep[0], deep[1] = list(got), list(got)

    def start_far(s, *after):
        operand = gate(sent[s], *after)[0] if after else sent[s]
        far[s] = [along_cls(operand, by) for by in shifts]

    def start_deep(s, *after):
        operand = gate(sent[s], *after)[0] if after else sent[s]
        deep[s] = [two_down(operand)]

    start_early()

    a_both, *factors = prepare(where, bounds, rates, increments, draw, crusher_rate, rows)
    *factors, fall_vec = factors
    lost_a = factors.pop(4)

    first = quarter * size
    mine, peer, mine_rest, peer_rest = local_terms(where, gate(occ, token, sent[0], sent[2])[0], lost_a, factors, first)
    _, got_rest = exchange(quarter, n, mine)
    far[0][0], _ = gate(far[0][0], mine)
    parts = [(0, quarter, 0, (mine, other_core(gate(peer, *far[0], *deep[0])[0])))]

    parts.append((quarter, n, first, (mine_rest, other_core(gate(peer_rest, parts[0][3][1])[0]))))
    offset = {1: size}
    out = None
    stay, rise, swap, lifted, risen = ([None] * n for _ in range(5))
    back = [None] * len(groups)
    group_of = {s: g for g, (lo, hi) in enumerate(groups) for s in range(lo, hi)}

    for s in range(n + 4):
        if s < n:
            if s == 2:
                far[2][0], _, _ = gate(far[2][0], got_rest, parts[1][3][1])
            if s >= 3:
                far[s][0], risen[s - 3] = gate(far[s][0], risen[s - 3])
            if s >= 4:
                far[s][0], out = gate(far[s][0], out)
            if s == 0:
                start_far(2, *far[0])
                start_deep(2, *far[0])
            elif 3 <= s + 1 < n and s != 1:
                start_far(s + 1, far[s][0])
            if 3 <= s + 2 < n:
                start_deep(s + 2, *deep[s])
            lo, hi, at, near = next(p for p in parts if p[0] <= s < p[1])
            stay[s], rise[s], swap[s] = first_terms(
                where,
                fall_vec,
                a_both,
                [(sent[s], 0)] + [(v, offset.get(s, 0)) for v in far[s]],
                [(v, offset.get(s, 0)) for v in deep[s]],
                near,
                chunks[s][0] - at,
                size,
            )
            lift_me = rise[s]
            if s >= 1:
                lift_me, lifted[s - 1] = gate(lift_me, lifted[s - 1])
            lifted[s] = two_up(lift_me)
        if 1 <= s <= n:
            p = s - 1
            swap_me = turn(swap[p], lifted[p])
            if p >= 1:
                swap_me, risen[p - 1] = gate(swap_me, risen[p - 1])
            risen[p] = pair_swap(swap_me)
        if 0 <= s - 2 < n:
            p = s - 2
            g = group_of[p]
            lo, hi = groups[g]
            out, back[g] = finish(
                where, out, back[g], occ.shape, (hi - lo) * size, stay[p], risen[p], chunks[p][0], (p - lo) * size
            )
            if p == hi - 1:
                back[g] = other_core(back[g])
        if 0 <= s - 3 < n:
            p = s - 3
            lo, hi = groups[group_of[p]]
            if p == hi - 1:
                out = put(where, out, back[group_of[p]], chunks[lo][0])
    return out[None]


def solution(mesh):
    in_specs = (P("lvl", "cls", None, None), P(), P(), P(), P(), P())
    out_specs = P("lvl", "cls", None, None)
    return jax.shard_map(local, mesh=mesh, in_specs=in_specs, out_specs=out_specs, check_vma=False)
```

```python
import functools

import jax
import jax.numpy as jnp
from jax import lax
from jax.experimental import pallas as pl
from jax.experimental.pallas import tpu as pltpu
from jax.sharding import PartitionSpec as P

F32 = jnp.float32
BF16 = jnp.bfloat16
VMEM_LIMIT = 56 * 2**20
SPAN, LANES = 8, 128
LIGHT = pl.CostEstimate(flops=1000, transcendentals=0, bytes_accessed=1000)
PARAMS = pltpu.CompilerParams(vmem_limit_bytes=VMEM_LIMIT)
WHOLE = pl.BlockSpec(memory_space=pltpu.VMEM)


def gate(*values):
    return lax.optimization_barrier(values)


def flag(cond):
    return jnp.where(cond, 1.0, 0.0).astype(F32)


def halves(x):
    high = x.astype(BF16)
    low = (x - high.astype(F32)).astype(BF16)
    return high, low


def halves_outside(x):
    high = lax.reduce_precision(x, 8, 7)
    return high.astype(BF16), (x - high).astype(BF16)


def dot(a, b):
    return jnp.dot(a, b, preferred_element_type=F32)


def plan(rows, length):
    n = max(4, rows // 4)
    size = length // n
    chunks = [(s * size, size) for s in range(n)]
    return chunks, [(0, n - 2), (n - 2, n - 1), (n - 1, n)]


def spans(*bounds):
    return list(zip(bounds[:-1], bounds[1:]))


def prepare_kernel(rows, where, bounds, rates, inc_rows, inc_cols, draw, crusher, a_out, c_hi, c_lo, b_hi, b_lo, lost_a, lost_b,
                   left_c, fall, flip):
    level = where[2]
    top, bottom = bounds[1], bounds[0]
    phases = rates.shape[1]
    totals = [jnp.sum(rates[c], axis=1, keepdims=True) for c in range(3)]
    uniform = jnp.max(crusher[...], axis=1, keepdims=True)
    for total in totals:
        uniform = uniform + jnp.max(total, axis=0, keepdims=True)
    scale = 1.0 / uniform
    rise_ok = jnp.where(level + 1 <= top, 1.0, 0.0)

    def opened(inc):
        return jnp.where((inc == 0) | (level + inc <= top), 1.0, 0.0)

    def masks(inc):
        return [jnp.where(inc == 0, 1.0, 0.0) * scale, jnp.where(inc == 1, 1.0, 0.0) * (rise_ok * scale)]

    lost_a[...] = totals[0] * opened(inc_cols[0]) * scale
    lost_b[...] = totals[1] * opened(inc_cols[1]) * scale
    total_c = jnp.sum(jnp.transpose(rates[2]), axis=0, keepdims=True)
    here = crusher[...] * jnp.where(level - draw[...] >= bottom, 1.0, 0.0)
    deep = crusher[...] * jnp.where(level + 2 - draw[...] >= bottom, 1.0, 0.0)
    left_c[...] = 1.0 - total_c * opened(inc_rows[2:3]) * scale - here * scale
    fall[0:1] = jnp.where(level % 2 == 0, deep, here) * jnp.where(draw[...] == 1, 1.0, 0.0) * scale
    fall[1:2] = deep * jnp.where(draw[...] == 2, 1.0, 0.0) * scale
    for n, mask in enumerate(masks(inc_cols[2])):
        high, low = halves(rates[2] * mask)
        c_hi[:, n * phases : (n + 1) * phases] = high
        c_lo[:, n * phases : (n + 1) * phases] = low
    for n, mask in enumerate(masks(inc_cols[1])):
        high, low = halves(jnp.transpose(rates[1] * mask))
        b_hi[n] = high
        b_lo[n] = low
    spots = [pl.ds(pl.multiple_of(where[3 + n] * rows, 8), rows) for n in range(phases // rows)]
    ordered = jnp.concatenate([rates[0, spot] for spot in spots], axis=0)
    inc = jnp.concatenate([inc_cols[0, spot] for spot in spots], axis=0)
    for n, mask in enumerate(masks(inc)):
        flip[...] = jnp.transpose(ordered * mask)
        for which in range(2):
            at = (2 * n + which) * rows
            high, low = halves(flip[spots[which]])
            a_out[at : at + rows] = high
            a_out[4 * rows + at : 5 * rows + at] = low


def prepare(where, bounds, rates, increments, draw, crusher_rate, rows):
    phases = rates.shape[1]
    smem = pl.BlockSpec(memory_space=pltpu.SMEM)
    shapes = [
        ((8 * rows, phases), BF16),
        ((phases, 2 * phases), BF16),
        ((phases, 2 * phases), BF16),
        ((2, phases, phases), BF16),
        ((2, phases, phases), BF16),
        ((phases, 1), F32),
        ((phases, 1), F32),
        ((1, phases), F32),
        ((2, phases), F32),
    ]
    return pl.pallas_call(
        functools.partial(prepare_kernel, rows),
        in_specs=[smem, smem] + [WHOLE] * 5,
        out_specs=[WHOLE] * len(shapes),
        out_shape=[jax.ShapeDtypeStruct(*v) for v in shapes],
        scratch_shapes=[pltpu.VMEM((phases, phases), F32)],
        compiler_params=PARAMS,
        cost_estimate=LIGHT,
        name="prepare",
    )(where, bounds, rates, increments, increments[:, :, None], draw[None], crusher_rate[None])


def local_kernel(half, where, lost_a, occ, c_hi, c_lo, b_hi, b_lo, lost_b, left_c, *outs):
    block, phases = occ.shape[0], occ.shape[2]
    mine, peer, mine_rest, peer_rest, b_both, left_b = outs
    size, cut = half, mine.shape[2]
    rows = [pl.ds(pl.multiple_of(where[n] * half, 16), size) for n in range(2)]

    @pl.when(pl.program_id(0) == 0)
    def _():
        for n in range(2):
            left_b[n * size : (n + 1) * size] = lost_b[rows[n]]
            for m in range(2):
                spot = (2 * m + n) * size
                b_both[spot : spot + size] = b_hi[m, rows[n]]
                b_both[4 * size + spot : 5 * size + spot] = b_lo[m, rows[n]]

    first = where[3] * (pl.num_programs(0) * block) + pl.program_id(0) * block
    y = jnp.concatenate([occ[i, r] for i in range(block) for r in rows], axis=0)
    y_hi, y_lo = halves(y)
    n_y = y.shape[0]
    by_c = dot(jnp.concatenate([y_hi, y_lo], axis=0), c_hi[...])
    by_c = by_c[:n_y] + by_c[n_y:] + dot(y_hi, c_lo[...])
    for i in range(block):
        x_hi, x_lo = halves(occ[i])
        by_b = dot(b_both[...], x_hi)
        by_b = by_b[: 4 * size] + by_b[4 * size :] + dot(b_both[: 4 * size], x_lo)
        here = slice(2 * size * i, 2 * size * (i + 1))
        left = left_c[...] - lost_a[pl.ds(first + i, 1)] - left_b[...]
        base = by_c[here, :phases] + by_b[: 2 * size] + y[here] * left
        rise = by_c[here, phases:] + by_b[2 * size :]
        for n, value in enumerate((base, rise)):
            mine[n, i] = value[:cut]
            mine_rest[n, i] = value[cut:size]
            peer[n, i] = value[size : size + cut]
            peer_rest[n, i] = value[size + cut :]


def local_terms(where, occ, lost_a, factors, first):
    rows, mid, phases = occ.shape
    block, size = 8, mid // 2
    sizes = [first, first, size - first, size - first]
    return pl.pallas_call(
        functools.partial(local_kernel, size),
        grid_spec=pltpu.PrefetchScalarGridSpec(
            num_scalar_prefetch=1,
            grid=(rows // block,),
            in_specs=[WHOLE, pl.BlockSpec((block, mid, phases), lambda i, c: (i, 0, 0))] + [WHOLE] * len(factors),
            out_specs=[pl.BlockSpec((2, block, v, phases), lambda i, c: (0, i, 0, 0)) for v in sizes],
            scratch_shapes=[pltpu.VMEM((8 * size, mid), BF16), pltpu.VMEM((2 * size, 1), F32)],
        ),
        out_shape=[jax.ShapeDtypeStruct((2, rows, v, phases), F32) for v in sizes],
        compiler_params=PARAMS,
        cost_estimate=LIGHT,
        name="local_terms",
    )(where, lost_a, occ, *factors)


def first_kernel(n_slabs, n_deep, where, fall, *refs):
    w_both = refs[0]
    slabs = refs[1 : 1 + n_slabs]
    deep = refs[1 + n_slabs : 1 + n_slabs + n_deep]
    mine, peer, stay_out, rise_out, swap_out = refs[1 + n_slabs + n_deep :]
    rows, span, lanes = stay_out.shape
    flat = [ref.reshape(ref.shape[0] * span, lanes) for ref in slabs]
    stay_flat = stay_out.reshape(rows * span, lanes)
    rise_flat = rise_out.reshape(rows * span, lanes)
    for b in range(0, span, 2):
        ats = [pl.ds(b, rows, stride=span), pl.ds(b + 1, rows, stride=span)]
        parts = []
        for ref in flat:
            picks = [pl.ds(b + n, ref.shape[0] // span, stride=span) for n in range(2)]
            parts.append(halves(jnp.concatenate([ref[pick, :] for pick in picks], axis=1)))
        g_hi = jnp.concatenate([p[0] for p in parts], axis=0)
        g_lo = jnp.concatenate([p[1] for p in parts], axis=0)
        both = dot(w_both[...], g_hi)
        out = both[: 2 * rows] + both[2 * rows :] + dot(w_both[: 2 * rows], g_lo)
        for n, at in enumerate(ats):
            stay_flat[at, :] = out[:rows, n * lanes : (n + 1) * lanes]
            rise_flat[at, :] = out[rows:, n * lanes : (n + 1) * lanes]
    half = rows // 2
    once, twice = fall[0:1], fall[1:2]
    for which, near in enumerate((mine, peer)):
        part = slice(which * half, (which + 1) * half)
        far_down = deep[which][...] if n_deep == 2 else deep[0][part]
        stay_out[part] += near[0] + far_down * twice
        lift = rise_out[part] + near[1]
        rise_out[part] = lift

        @pl.when(where[2] % 2 == 0)
        def _():
            swap_out[part] = lift + far_down * once

    @pl.when(where[2] % 2 != 0)
    def _():
        at = 0
        for ref in slabs:
            if at < rows:
                swap_out[at : at + ref.shape[0]] = ref[...] * once
            at += ref.shape[0]


def first_terms(where, fall, w_both, slabs, deep, near, start, size):
    rows, _, phases = slabs[0][0].shape
    slab_specs = [
        pl.BlockSpec((v.shape[0], SPAN, LANES), lambda j, h, at=at: (0, at // SPAN + j, h)) for v, at in [*slabs, *deep]
    ]
    chunk = pl.BlockSpec((rows, SPAN, LANES), lambda j, h: (0, j, h))
    local_part = pl.BlockSpec((2, rows // 2, SPAN, LANES), lambda j, h: (0, 0, start // SPAN + j, h))
    return pl.pallas_call(
        functools.partial(first_kernel, len(slabs), len(deep)),
        grid=(size // SPAN, phases // LANES),
        in_specs=[pl.BlockSpec(memory_space=pltpu.SMEM), pl.BlockSpec((2, LANES), lambda j, h: (0, h)), WHOLE]
        + slab_specs
        + [local_part] * 2,
        out_specs=[chunk] * 3,
        out_shape=[jax.ShapeDtypeStruct((rows, size, phases), F32)] * 3,
        compiler_params=PARAMS,
        cost_estimate=LIGHT,
        name="first_terms",
    )(where, fall, w_both, *[v for v, _ in [*slabs, *deep]], *near)


def turn_kernel(swap, lifted, out):
    out[...] = swap[...] + lifted[...]


def turn(swap, lifted):
    rows, size, phases = swap.shape
    block = max(8, rows // 2)
    chunk = pl.BlockSpec((block, SPAN, phases), lambda i, j: (i, j, 0))
    return pl.pallas_call(
        turn_kernel,
        grid=(rows // block, size // SPAN),
        in_specs=[chunk, chunk],
        out_specs=chunk,
        out_shape=jax.ShapeDtypeStruct(swap.shape, F32),
        compiler_params=PARAMS,
        cost_estimate=LIGHT,
        name="turn",
    )(swap, lifted)


def finish_kernel(n_alias, _, *refs):
    out, back = refs[4 + n_alias :]
    out[...] = refs[0][...] + refs[1][...]
    back[...] = refs[2][...] + refs[3][...]


def finish(core, out, back, shape, back_size, stay, risen, start, back_at):
    rows, size, phases = stay.shape
    half = rows // 2
    steps = shape[1] // 2 // SPAN
    args, specs = [core], []
    for which in range(2):
        for array in (stay, risen):
            args.append(array)
            specs.append(pl.BlockSpec((half, SPAN, LANES), lambda j, h, c, which=which: (which, j, h)))
    alias = {}
    for n, old in enumerate((out, back)):
        if old is not None:
            alias[len(args)] = n
            args.append(old)
            specs.append(pl.BlockSpec(memory_space=pl.ANY))
    return pl.pallas_call(
        functools.partial(finish_kernel, len(alias)),
        grid_spec=pltpu.PrefetchScalarGridSpec(
            num_scalar_prefetch=1,
            grid=(size // SPAN, phases // LANES),
            in_specs=specs,
            out_specs=[
                pl.BlockSpec((half, SPAN, LANES), lambda j, h, c: (0, c[0] * steps + start // SPAN + j, h)),
                pl.BlockSpec((half, SPAN, LANES), lambda j, h, c: (0, back_at // SPAN + j, h)),
            ],
        ),
        out_shape=[jax.ShapeDtypeStruct(shape, F32), jax.ShapeDtypeStruct((half, back_size, phases), F32)],
        input_output_aliases=alias,
        compiler_params=PARAMS,
        cost_estimate=LIGHT,
        name="finish",
    )(*args)


def put_kernel(core, piece, _, out):
    out[...] = piece[...]


def put(core, out, piece, start):
    rows, size, phases = piece.shape
    steps = out.shape[1] // 2 // SPAN
    return pl.pallas_call(
        put_kernel,
        grid_spec=pltpu.PrefetchScalarGridSpec(
            num_scalar_prefetch=1,
            grid=(size // SPAN,),
            in_specs=[
                pl.BlockSpec((rows, SPAN, phases), lambda j, c: (0, j, 0)),
                pl.BlockSpec(memory_space=pl.ANY),
            ],
            out_specs=pl.BlockSpec((rows, SPAN, phases), lambda j, c: (0, c[1] * steps + start // SPAN + j, 0)),
        ),
        out_shape=jax.ShapeDtypeStruct(out.shape, F32),
        input_output_aliases={2: 0},
        compiler_params=PARAMS,
        cost_estimate=LIGHT,
        name="put",
    )(core, piece, out)


def local(occupancy, rates, increments, draw, crusher_rate, bounds):
    n_cls, n_lvl = lax.axis_size("cls"), lax.axis_size("lvl")
    occ = occupancy[0]
    rows, mid, phases = occ.shape
    half = mid // 2
    level = lax.axis_index("lvl")
    place = lax.axis_index("cls")
    k = place % 2
    core = (k, 1 - k)
    origin = [place, place ^ 1]
    for by in range(2, n_cls, 2):
        origin += [(place - by) % n_cls, ((place - by) % n_cls) ^ 1]
    where = jnp.stack([*core, level, *origin])

    def along_cls(v, by):
        return lax.ppermute(v, "cls", [(i, (i + by) % n_cls) for i in range(n_cls)])

    def other_core(v):
        return lax.ppermute(v, "cls", [(i, i ^ 1) for i in range(n_cls)])

    def two_down(v):
        return lax.ppermute(v, "lvl", [(i, i - 2) for i in range(2, n_lvl)])

    def two_up(v):
        return lax.ppermute(v, "lvl", [(i, i + 2) for i in range(1, n_lvl - 2, 2)])

    def pair_swap(v):
        return lax.ppermute(v, "lvl", [(i, i ^ 1) for i in range(n_lvl)])

    def cut(array, which, at, size):
        return lax.dynamic_slice_in_dim(array, core[which] * half + at, size, axis=1)

    chunks, groups = plan(rows, half)
    n = len(chunks)
    size = chunks[0][1]
    shifts = [2 * s for s in range(1, n_cls // 2)]
    sent = [None] * n

    def exchange(lo, hi, *after):
        at = chunks[lo][0]
        give = cut(occ, 1, at, (hi - lo) * size)
        if after:
            give = gate(give, *after)[0]
        got = other_core(give)
        for s in range(lo, hi):
            start = chunks[s][0]
            part = lax.slice_in_dim(got, start - at, start - at + size, axis=1)
            sent[s] = jnp.concatenate([cut(occ, 0, start, size), part], axis=0)
        return give, got

    quarter = max(3, n // 4)
    _, token = exchange(0, quarter)
    give_rest, got_rest = exchange(quarter, n, sent[0])

    far, deep = [None] * n, [None] * n

    def start_early():
        own, other = cut(occ, 0, 0, 2 * size), cut(occ, 1, 0, 2 * size)
        got = []
        for by in shifts:
            crossed = [(i, ((i + by) % n_cls) ^ 1) for i in range(n_cls)]
            got += [along_cls(own, by), lax.ppermute(other, "cls", crossed)]
        far[0], far[1] = list(got), list(got)
        both = [(i * n_lvl + m, (i ^ 1) * n_lvl + m - 2) for i in range(n_cls) for m in range(2, n_lvl)]
        got = [two_down(own), lax.ppermute(other, ("cls", "lvl"), both)]
        deep[0], deep[1] = list(got), list(got)

    def start_far(s, *after):
        operand = gate(sent[s], *after)[0] if after else sent[s]
        far[s] = [along_cls(operand, by) for by in shifts]

    def start_deep(s, *after):
        operand = gate(sent[s], *after)[0] if after else sent[s]
        deep[s] = [two_down(operand)]

    start_early()

    a_both, *factors = prepare(where, bounds, rates, increments, draw, crusher_rate, rows)
    *factors, fall_vec = factors
    lost_a = factors.pop(4)

    first = quarter * size
    mine, peer, mine_rest, peer_rest = local_terms(where, gate(occ, token, sent[0], sent[2], give_rest)[0], lost_a, factors, first)
    far[0][0], _ = gate(far[0][0], mine)
    parts = [(0, quarter, 0, (mine, other_core(gate(peer, *far[0], *deep[0])[0])))]

    parts.append((quarter, n, first, (mine_rest, other_core(gate(peer_rest, parts[0][3][1])[0]))))
    offset = {1: size}
    out = None
    stay, rise, swap, lifted, risen = ([None] * n for _ in range(5))
    back = [None] * len(groups)
    group_of = {s: g for g, (lo, hi) in enumerate(groups) for s in range(lo, hi)}

    for s in range(n + 4):
        if s < n:
            if s == 2:
                far[2][0], _, _ = gate(far[2][0], got_rest, parts[1][3][1])
            if s >= 3:
                far[s][0], risen[s - 3] = gate(far[s][0], risen[s - 3])
            if s >= 4:
                far[s][0], out = gate(far[s][0], out)
            if s == 0:
                start_far(2, *far[0])
                start_deep(2, *far[0])
            elif 3 <= s + 1 < n and s != 1:
                start_far(s + 1, far[s][0])
            if 3 <= s + 2 < n:
                start_deep(s + 2, *deep[s])
            lo, hi, at, near = next(p for p in parts if p[0] <= s < p[1])
            stay[s], rise[s], swap[s] = first_terms(
                where,
                fall_vec,
                a_both,
                [(sent[s], 0)] + [(v, offset.get(s, 0)) for v in far[s]],
                [(v, offset.get(s, 0)) for v in deep[s]],
                near,
                chunks[s][0] - at,
                size,
            )
            lift_me = rise[s]
            if s >= 1:
                lift_me, lifted[s - 1] = gate(lift_me, lifted[s - 1])
            lifted[s] = two_up(lift_me)
        if 1 <= s <= n:
            p = s - 1
            swap_me = turn(swap[p], lifted[p])
            if p >= 1:
                swap_me, risen[p - 1] = gate(swap_me, risen[p - 1])
            risen[p] = pair_swap(swap_me)
        if 0 <= s - 2 < n:
            p = s - 2
            g = group_of[p]
            lo, hi = groups[g]
            out, back[g] = finish(
                where, out, back[g], occ.shape, (hi - lo) * size, stay[p], risen[p], chunks[p][0], (p - lo) * size
            )
            if p == hi - 1:
                back[g] = other_core(back[g])
        if 0 <= s - 3 < n:
            p = s - 3
            lo, hi = groups[group_of[p]]
            if p == hi - 1:
                out = put(where, out, back[group_of[p]], chunks[lo][0])
    return out[None]


def solution(mesh):
    in_specs = (P("lvl", "cls", None, None), P(), P(), P(), P(), P())
    out_specs = P("lvl", "cls", None, None)
    return jax.shard_map(local, mesh=mesh, in_specs=in_specs, out_specs=out_specs, check_vma=False)
```
